768 devices in a mesh: member: 16 (over z_hi, x), space: 48 (over z_lo, y, core).
Axes of the slice: x: 4, y: 8, z: 12 (z_hi: 4, z_lo: 3; z = z_hi * 3 + z_lo), core: 2. Of those that a mesh axis runs over, the one named last changes fastest.
Arguments:
- perturb: float32 [16, 192, 96, 192], P('member', 'space'), may hold values from -8 to 8
- register: float32 [16, 192, 18432], P('member', 'space'), may hold values from -6 to 6
- ref_velocity: float32 [3, 192, 192], P(None, 'space', 'member'), may hold values from -6 to 6
Outputs:
- advanced_perturb: float32 [16, 192, 18432], P('member', 'space')
- advanced_register: float32 [16, 192, 18432], P('member', 'space')
- reference_step: float32 [3, 192, 192], P(None, 'member', 'space')
- gram: float32 [16, 16], P('member')
The draws below stay inside these ranges and needn't reach their ends.
All inputs are finite; a program needn't handle non-finite values.
Results may differ from the reference program's by a relative error of at most 0.00012.
Values sent between devices are 32-bit elements; how exact they have to be, the bound alone decides.
A program may use at most 32 MiB of HBM per device.

```python
import jax
import jax.numpy as jnp
import numpy as np
from jax import lax

NY = 192
NZ = 192
KX = 16
CH = 96
MEMBERS = 16


def draw_perturb(key, part):
    keys = jax.random.split(key, 5)
    common = jnp.clip(jax.random.normal(keys[1], (1, NY, CH, NZ), jnp.float32), -4.0, 4.0)
    own_part = jnp.clip(jax.random.normal(keys[2], (MEMBERS, NY, CH, NZ), jnp.float32), -4.0, 4.0)
    signs = jnp.where(jax.random.bernoulli(keys[3], 0.5, (MEMBERS, 1, 1, 1)), 1.0, -1.0).astype(jnp.float32)
    mixing = jax.random.uniform(keys[4], (MEMBERS, 2, 1, 1, 1), jnp.float32, 0.6, 1.0)
    return signs * mixing[:, 0] * common + mixing[:, 1] * own_part


def shard_levels(rng, extent, cuts, smallest, largest):
    def one(position, blocks):
        steps = jax.random.uniform(jax.random.fold_in(jax.random.fold_in(rng, 6), position), (blocks,), jnp.float32, smallest / len(cuts), largest / len(cuts))
        return jnp.repeat(jnp.exp(steps), extent[position] // blocks).reshape((-1,) + (1,) * (len(extent) - position - 1))

    factor_of = one(*cuts[0])
    for cut in cuts[1:]:
        factor_of = factor_of * one(*cut)
    return factor_of


def noise(stream_key, extent, scale, bound, shards=(), kind=jnp.bfloat16):
    result = jax.random.normal(stream_key, extent, jnp.float32) * scale
    if len(shards) > 0:
        result = shard_levels(stream_key, extent, shards, -0.22, 0.18) * result
    return jnp.clip(result, min=-bound, max=bound).astype(kind)


def setup_inputs(seed: int = 0) -> dict:
    streams_of = jax.random.split(jax.random.key(seed), 4)
    return {
        "perturb": draw_perturb(jax.random.fold_in(streams_of[3], 71), 0),
        "register": noise(streams_of[1], (MEMBERS, NZ, NY * CH), 0.5, 6.0, ((0, 16), (1, 48)), jnp.float32),
        "ref_velocity": noise(streams_of[2], (3, NY, NZ), 1.0, 6.0, ((1, 48), (2, 16)), jnp.float32),
    }


time_step = 2e-5
alpha_coef = -5.0 / 9.0
beta_coef = 15.0 / 16.0
lorentz_rate = 25.0
wave_step = 0.5


def cheb_matrix(points):
    intervals = points - 1
    index = np.arange(points)
    nodes = np.cos(np.pi * index / intervals)
    signs = np.ones(points)
    signs[0] = 2.0
    signs[-1] = 2.0
    signs = signs * (-1.0) ** index
    spread = nodes[:, None] - nodes[None, :]
    matrix = (signs[:, None] / signs[None, :]) / (spread + np.eye(points))
    matrix = matrix - np.eye(points) * matrix.sum(axis=1)[:, None]
    return matrix


def quad_weights(points):
    index = np.arange(points)
    return np.pi / (points - 1) * np.sin(np.pi * index / (points - 1))


def interior(points):
    index = jnp.arange(points)
    return ((index > 0) & (index < points - 1)).astype(jnp.float32)


def reference(perturb, register, ref_velocity):
    highest = lax.Precision.HIGHEST
    dy_mat = jnp.asarray(cheb_matrix(NY), jnp.float32)
    dz_mat = jnp.asarray(cheb_matrix(NZ), jnp.float32)
    dy_ref = jnp.einsum('wy,cyz->cwz', dy_mat, ref_velocity, precision=highest)
    dz_ref = jnp.einsum('cyz,wz->cyw', ref_velocity, dz_mat, precision=highest)
    vel_u = ref_velocity[0]
    vel_v = ref_velocity[1][:, None, None, None, :]
    vel_w = ref_velocity[2][:, None, None, None, :]
    stream_u = vel_u[:, None, None, :]
    dy_ref_b = jnp.transpose(dy_ref, (1, 0, 2))[:, None, None, :, :]
    dz_ref_b = jnp.transpose(dz_ref, (1, 0, 2))[:, None, None, :, :]
    mask_two = interior(NY)[:, None] * interior(NZ)[None, :]
    mask_five = mask_two[:, None, None, None, :]
    waves = ((jnp.arange(KX) + 1).astype(jnp.float32) * wave_step).reshape(1, KX, 1, 1)
    lorentz = jnp.array([1.0, 0.0, 1.0], jnp.float32).reshape(1, 1, 1, 3, 1)
    reg_std = jnp.transpose(register.reshape(MEMBERS, NZ, NY, CH), (0, 2, 3, 1))

    def member(pair):
        field, acc = pair
        five = field.reshape(NY, KX, 2, 3, NZ)
        dzq = jnp.einsum('ycz,wz->ycw', field, dz_mat, precision=highest).reshape(NY, KX, 2, 3, NZ)
        dyq = jnp.einsum('wy,ycz->wcz', dy_mat, field, precision=highest).reshape(NY, KX, 2, 3, NZ)
        twist = jnp.stack([waves * stream_u * five[:, :, 1], -waves * stream_u * five[:, :, 0]], axis=2)
        zpart = -vel_w * dzq - five[:, :, :, 2:3] * dz_ref_b
        rhs = zpart + (-vel_v * dyq + twist - five[:, :, :, 1:2] * dy_ref_b - lorentz_rate * lorentz * five)
        acc_new = mask_five * (alpha_coef * acc.reshape(NY, KX, 2, 3, NZ) + time_step * rhs)
        field_new = mask_five * (five + beta_coef * acc_new)
        return field_new.reshape(NY, CH, NZ), acc_new.reshape(NY, CH, NZ)

    fields, accs = lax.map(member, (perturb, reg_std))
    weight_y = jnp.asarray(quad_weights(NY), jnp.float32)
    weight_z = jnp.asarray(quad_weights(NZ), jnp.float32)
    weighted = fields * weight_y[None, :, None, None] * weight_z[None, None, None, :]
    gram = jnp.einsum('mycz,nycz->mn', weighted, fields, precision=highest) / CH
    lorentz_three = jnp.array([1.0, 0.0, 1.0], jnp.float32).reshape(3, 1, 1)
    rhs_ref = (-ref_velocity[2][None] * dz_ref) + (-ref_velocity[1][None] * dy_ref - lorentz_rate * lorentz_three * ref_velocity)
    ref_step = time_step * mask_two[None] * rhs_ref
    fields_out = jnp.transpose(fields, (0, 3, 1, 2)).reshape(MEMBERS, NZ, NY * CH)
    accs_out = jnp.transpose(accs, (0, 3, 1, 2)).reshape(MEMBERS, NZ, NY * CH)
    return fields_out, accs_out, ref_step, gram
```

```python
import functools

import jax
import jax.numpy as jnp
import numpy as np
from jax import lax
from jax.experimental import pallas as pl
from jax.experimental.pallas import tpu as pltpu
from jax.sharding import PartitionSpec as P

MESH = pl.DeviceIdType.MESH
HIGHEST = lax.Precision.HIGHEST

time_step = 2e-05
alpha_coef = -5.0 / 9.0
beta_coef = 15.0 / 16.0
lorentz_rate = 25.0
wave_step = 0.5

CH = 96
LANES = 128
SLOT = 40


def cheb_matrix(points):
    intervals = points - 1
    index = np.arange(points)
    nodes = np.cos(np.pi * index / intervals)
    signs = np.ones(points)
    signs[0] = 2.0
    signs[-1] = 2.0
    signs = signs * (-1.0) ** index
    spread = nodes[:, None] - nodes[None, :]
    matrix = signs[:, None] / signs[None, :] / (spread + np.eye(points))
    matrix = matrix - np.eye(points) * matrix.sum(axis=1)[:, None]
    return matrix


def quad_weights(points):
    index = np.arange(points)
    return np.pi / (points - 1) * np.sin(np.pi * index / (points - 1))


def constants(space, members):
    points = 4 * space
    diff = cheb_matrix(points).astype(np.float32)
    both = np.stack([np.eye(points, dtype=np.float32), diff]).reshape(2, space, 4, points)
    both = both.transpose(1, 0, 2, 3).reshape(2 * points, points)
    weight = quad_weights(points)
    lane_y = np.repeat(weight, CH).reshape(members, 9, LANES)
    lane_w = np.zeros((members, 16, LANES), np.float32)
    lane_w[:, :9] = lane_y
    return both, diff, lane_w, weight.astype(np.float32)


def mm(a, b, transpose_b=False):
    dims = (((1,), (1 if transpose_b else 0,)), ((), ()))
    return lax.dot_general(a, b, dims, precision=HIGHEST, preferred_element_type=jnp.float32)


def iota(shape, axis):
    return lax.broadcasted_iota(jnp.int32, shape, axis)


def kernel(
    S,
    M,
    p_ref,
    reg_ref,
    v_ref,
    a_ref,
    dy_ref,
    wl_ref,
    wz_ref,
    outf_ref,
    outa_ref,
    outr_ref,
    outg_ref,
    send_b,
    recv_b,
    tpose,
    own_x,
    gath_x,
    xz,
    ct,
    send_c,
    recv_c,
    coef,
    sbuf,
    tbuf,
    rbuf,
    f_loc,
    a_loc,
    f_buf,
    g_buf,
    gp,
    gr,
    row,
    rows,
    send_sem,
    recv_sem,
    out_sem,
):
    N = 4 * S
    H = S // 2
    m = lax.axis_index("member")
    s = lax.axis_index("space")

    def over_space(body):
        def step(k, carry):
            body(lax.rem(s + k, S))
            return carry

        lax.fori_loop(1, S, step, 0)

    def over_member(body):
        def step(k, carry):
            body(lax.rem(m + k, M))
            return carry

        lax.fori_loop(1, M, step, 0)

    def push(src, dst, which, member, space):
        pltpu.make_async_remote_copy(
            src_ref=src,
            dst_ref=dst,
            send_sem=send_sem.at[which],
            recv_sem=recv_sem.at[which],
            device_id=(member, space),
            device_id_type=MESH,
        ).start()

    def keep(src, dst, which):
        pltpu.make_async_copy(src, dst, recv_sem.at[which]).start()

    def arrived(ref, which):
        pltpu.make_async_copy(ref, ref, recv_sem.at[which]).wait()

    def sent(ref, which):
        pltpu.make_async_copy(ref, ref, send_sem.at[which]).wait()

    barrier = pltpu.get_barrier_semaphore()
    over_space(
        lambda t: pl.semaphore_signal(barrier, inc=1, device_id=(m, t), device_id_type=MESH)
    )
    over_member(
        lambda t: pl.semaphore_signal(barrier, inc=1, device_id=(t, s), device_id_type=MESH)
    )

    tpose[...] = jnp.zeros((LANES, LANES), jnp.float32)
    for c in range(3):
        tpose[4 * c : 4 * c + 4, 0:12] = v_ref[c]
    tpose[...] = tpose[...].T
    own_x[...] = (
        tpose[0:4, :]
        + pltpu.roll(tpose[4:8, :], 12, 1)
        + pltpu.roll(tpose[8:12, :], 24, 1)
    )
    send_b[...] = mm(a_ref[...], p_ref[...], transpose_b=True)

    pl.semaphore_wait(barrier, S - 1 + M - 1)

    over_member(lambda t: push(own_x, gath_x.at[m], 0, t, s))
    keep(own_x, gath_x.at[m], 0)

    def bulk(t):
        push(
            send_b.at[pl.ds(pl.multiple_of(8 * t, 8), 8), :],
            recv_b.at[pl.ds(pl.multiple_of(8 * s, 8), 8), :],
            1,
            m,
            t,
        )

    over_space(bulk)
    mine = pl.ds(pl.multiple_of(8 * s, 8), 8)
    keep(send_b.at[mine, :], recv_b.at[mine, :], 1)

    arrived(gath_x, 0)
    for k in range(M):
        piece = gath_x[k]
        for j in range(3):
            part = piece if j == 0 else pltpu.roll(piece, LANES - 12 * j, 1)
            xz[12 * k + 4 * j : 12 * k + 4 * j + 4, :] = part
    x = jnp.where(iota((N, LANES), 1) < 12, xz[...], 0.0)
    ct[...] = mm(a_ref[...], x)
    packed = ct[pl.ds(0, S, stride=8), :]
    for k in range(1, 8):
        packed = packed + pltpu.roll(ct[pl.ds(k, S, stride=8), :], 12 * k, 1)
    send_c[:, 0, :] = packed
    over_space(lambda t: push(send_c.at[t], recv_c.at[s], 2, m, t))
    keep(send_c.at[s], recv_c.at[s], 2)

    arrived(recv_c, 2)
    spread = (iota((N, S), 0) // 4 == iota((N, S), 1)).astype(jnp.float32)
    wide = mm(spread, recv_c[:, 0, :])
    points = jnp.where(iota((N, LANES), 1) % 4 == iota((N, LANES), 0) % 4, wide, 0.0)
    dpoints = mm(dy_ref[...], points)
    group = iota((LANES, LANES), 0) // 4
    lane = iota((LANES, LANES), 1)
    comp = lane % 3
    kx = wave_step * (lane // 6 + 1).astype(jnp.float32)
    kx = jnp.where(lane % 6 < 3, kx, -kx)
    lane_n = iota((N, LANES), 1)
    lorentz = jnp.where(lane_n % 3 == 1, 0.0, lorentz_rate)
    pick = (iota((16, N), 1) == 12 * m + iota((16, N), 0)).astype(jnp.float32)
    ref_rows = jnp.zeros((16, LANES), jnp.float32)
    for z in range(4):
        sel = [
            (group == 3 * z + 2).astype(jnp.float32),
            (group == 3 * z + 1).astype(jnp.float32),
            jnp.where(group == 3 * z, kx, 0.0),
            (group == 12 + 3 * z + comp).astype(jnp.float32),
            (group == 3 * z + comp).astype(jnp.float32),
        ]
        cw = mm(points, sel[0])
        cv = mm(points, sel[1])
        cu = mm(points, sel[2])
        cz = mm(points, sel[3])
        cr = mm(points, sel[4])
        cy = mm(dpoints, sel[4])
        coef[0, z] = cw
        coef[1, z] = cv
        coef[2, z] = cu
        coef[3, z] = cz
        coef[4, z] = cy
        ref_rhs = -cw * cz + (-cv * cy - lorentz * cr)
        got = mm(pick, ref_rhs)
        ref_rows = ref_rows + pltpu.roll(jnp.where(iota((16, LANES), 1) < 3, got, 0.0), 4 * z, 1)
    tpose[...] = jnp.zeros((LANES, LANES), jnp.float32)
    tpose[0:16, :] = ref_rows
    tpose[...] = tpose[...].T
    y_row = 12 * m + iota((1, 12), 1)
    for z in range(4):
        z_row = 4 * s + z
        inside = (y_row > 0) & (y_row < N - 1) & (z_row > 0) & (z_row < N - 1)
        for c in range(3):
            value = tpose[4 * z + c : 4 * z + c + 1, 0:12]
            outr_ref[c, z : z + 1, :] = time_step * jnp.where(inside, value, 0.0)

    arrived(recv_b, 1)
    lane8 = iota((8, LANES), 1)

    def expand(r, carry):
        base = pl.ds(pl.multiple_of(8 * r, 8), 8)
        v0 = recv_b[base, 0:128]
        v1 = recv_b[base, 128:256]
        v2 = recv_b[base, 256:384]
        y1 = jnp.where(lane8 < 32, pltpu.roll(v0, 32, 1), pltpu.roll(v1, 32, 1))
        y2 = jnp.where(lane8 < 64, pltpu.roll(v1, 64, 1), pltpu.roll(v2, 64, 1))
        y3 = pltpu.roll(v2, 96, 1)
        for i, v in enumerate((v0, y1, y2, y3)):
            sbuf[pl.ds(pl.multiple_of(32 * r + 8 * i, 8), 8), :] = v
        return carry

    lax.fori_loop(0, S, expand, 0)
    real = lane_n % 6 < 3
    comp_n = lane_n % 3
    half = N // 2
    for pair in range(2):
        q2 = jnp.concatenate(
            [sbuf[pl.ds(2 * pair + i, N, stride=8), :] for i in range(2)], axis=1
        )
        dyq2 = mm(dy_ref[...], q2)
        for i in range(2):
            z = 2 * pair + i
            q = q2[:, LANES * i : LANES * (i + 1)]
            dyq = dyq2[:, LANES * i : LANES * (i + 1)]
            dzq = sbuf[pl.ds(4 + z, N, stride=8), :]
            up1 = pltpu.roll(q, LANES - 1, 1)
            up2 = pltpu.roll(q, LANES - 2, 1)
            down1 = pltpu.roll(q, 1, 1)
            qz = jnp.where(comp_n == 0, up2, jnp.where(comp_n == 1, up1, q))
            qy = jnp.where(comp_n == 0, up1, jnp.where(comp_n == 1, q, down1))
            other = jnp.where(real, pltpu.roll(q, LANES - 3, 1), pltpu.roll(q, 3, 1))
            rhs = (-coef[0, z] * dzq - qz * coef[3, z]) + (
                -coef[1, z] * dyq + coef[2, z] * other - qy * coef[4, z] - lorentz * q
            )
            tbuf[pl.ds(z, half, stride=8), :] = rhs[0:half]
            tbuf[pl.ds(4 + z, half, stride=8), :] = rhs[half:N]

    def compact(r, carry):
        t = [tbuf[pl.ds(pl.multiple_of(32 * r + 8 * i, 8), 8), :] for i in range(4)]
        t1 = pltpu.roll(t[1], 96, 1)
        t2 = pltpu.roll(t[2], 64, 1)
        t3 = pltpu.roll(t[3], 32, 1)
        rbuf[r, :, 0:128] = jnp.where(lane8 < 96, t[0], t1)
        rbuf[r, :, 128:256] = jnp.where(lane8 < 64, t1, t2)
        rbuf[r, :, 256:384] = jnp.where(lane8 < 32, t2, t3)
        return carry

    lax.fori_loop(0, H, compact, 0)
    z_rows = 4 * s + iota((4, 384), 0)
    z_mask = (z_rows > 0) & (z_rows < N - 1)
    lane_y = iota((4, 384), 1) // CH

    def finish(g, carry):
        for h in range(2):
            slot = h * (S // 6) + g
            base = pl.multiple_of(SLOT * slot, 8)
            for i in range(3):
                r = h * H + 3 * g + i
                at = pl.ds(pl.multiple_of(384 * r, 128), 384)
                y = 4 * r + lane_y
                mask = jnp.where(z_mask & (y > 0) & (y < N - 1), 1.0, 0.0)
                rhs = rbuf[3 * g + i, 4 * h : 4 * h + 4, :]
                q = recv_b[pl.ds(pl.multiple_of(8 * r, 8), 4), :]
                acc = mask * (alpha_coef * reg_ref[:, at] + time_step * rhs)
                field = mask * (q + beta_coef * acc)
                a_loc[:, at] = acc
                f_loc[:, at] = field
                for l in range(3):
                    f_buf[pl.ds(base + 12 * i + 4 * l, 4), :] = field[:, 128 * l : 128 * l + 128]
        return carry

    lax.fori_loop(0, S // 6, finish, 0)

    def slot_of(t):
        return pl.ds(pl.multiple_of(SLOT * t, 8), SLOT)

    over_member(lambda t: push(f_buf.at[slot_of(t), :], g_buf.at[slot_of(m), :], 3, t, s))
    keep(f_buf.at[slot_of(m), :], g_buf.at[slot_of(m), :], 3)
    out_f = pltpu.make_async_copy(f_loc, outf_ref, out_sem.at[0])
    out_a = pltpu.make_async_copy(a_loc, outa_ref, out_sem.at[1])
    out_f.start()
    out_a.start()
    gp[...] = jnp.zeros((M, 1, LANES), jnp.float32)
    arrived(g_buf, 3)
    left = []
    right = []
    for t in range(9):
        weight_y = wl_ref[m, t : t + 1, :]
        for z in range(4):
            value = g_buf[pl.ds(4 * t + z, M, stride=SLOT), :]
            right.append(value)
            left.append(value * (weight_y * wz_ref[4 * s + z]))
    part = mm(jnp.concatenate(left, axis=1), jnp.concatenate(right, axis=1), transpose_b=True)
    for k in range(M):
        gp[k, :, 0:M] = part[k : k + 1, :]
    over_member(lambda t: push(gp.at[t], gr.at[m], 4, t, s))
    keep(gp.at[m], gr.at[m], 4)
    arrived(gr, 4)
    row[...] = jnp.sum(gr[...], axis=0)
    over_space(lambda t: push(row, rows.at[s], 5, m, t))
    keep(row, rows.at[s], 5)
    arrived(rows, 5)
    outg_ref[...] = (jnp.sum(rows[...], axis=0) / CH)[:, 0:M]

    sent(gath_x.at[0 : M - 1], 0)
    sent(recv_b.at[0 : 8 * (S - 1), :], 1)
    sent(recv_c.at[0 : S - 1], 2)
    sent(g_buf.at[0 : SLOT * (M - 1), :], 3)
    sent(gr.at[0 : M - 1], 4)
    sent(rows.at[0 : S - 1], 5)
    out_f.wait()
    out_a.wait()


def shards(S, M, perturb, register, ref_velocity):
    N = 4 * S
    f32 = jnp.float32
    both, diff, lane_w, weight = constants(S, M)
    vmem = pl.BlockSpec(memory_space=pltpu.VMEM)
    smem = pl.BlockSpec(memory_space=pltpu.SMEM)
    hbm = pl.BlockSpec(memory_space=pl.ANY)
    outs = pl.pallas_call(
        functools.partial(kernel, S, M),
        out_shape=(
            jax.ShapeDtypeStruct((4, N * CH), f32),
            jax.ShapeDtypeStruct((4, N * CH), f32),
            jax.ShapeDtypeStruct((3, 4, 12), f32),
            jax.ShapeDtypeStruct((1, M), f32),
        ),
        in_specs=[vmem] * 6 + [smem],
        out_specs=(hbm, hbm, vmem, vmem),
        scratch_shapes=[
            pltpu.VMEM((2 * N, 384), f32),
            pltpu.VMEM((2 * N, 384), f32),
            pltpu.VMEM((LANES, LANES), f32),
            pltpu.VMEM((4, LANES), f32),
            pltpu.VMEM((M, 4, LANES), f32),
            pltpu.VMEM((N, LANES), f32),
            pltpu.VMEM((2 * N, LANES), f32),
            pltpu.VMEM((S, 1, LANES), f32),
            pltpu.VMEM((S, 1, LANES), f32),
            pltpu.VMEM((5, 4, N, LANES), f32),
            pltpu.VMEM((8 * N, LANES), f32),
            pltpu.VMEM((4 * N, LANES), f32),
            pltpu.VMEM((S // 2, 8, 384), f32),
            pltpu.VMEM((4, N * CH), f32),
            pltpu.VMEM((4, N * CH), f32),
            pltpu.VMEM((SLOT * M, LANES), f32),
            pltpu.VMEM((SLOT * M, LANES), f32),
            pltpu.VMEM((M, 1, LANES), f32),
            pltpu.VMEM((M, 1, LANES), f32),
            pltpu.VMEM((1, LANES), f32),
            pltpu.VMEM((S, 1, LANES), f32),
            pltpu.SemaphoreType.DMA((6,)),
            pltpu.SemaphoreType.DMA((6,)),
            pltpu.SemaphoreType.DMA((2,)),
        ],
        compiler_params=pltpu.CompilerParams(collective_id=0, has_side_effects=True),
        name="substep",
    )(
        perturb.reshape(4 * CH, N),
        register[0],
        ref_velocity,
        jnp.asarray(both),
        jnp.asarray(diff),
        jnp.asarray(lane_w),
        jnp.asarray(weight),
    )
    fields, acc, ref_step, gram = outs
    return fields[None], acc[None], jnp.transpose(ref_step, (0, 2, 1)), gram


def solution(mesh):
    return jax.shard_map(
        functools.partial(shards, mesh.shape["space"], mesh.shape["member"]),
        mesh=mesh,
        in_specs=(
            P("member", "space", None, None),
            P("member", "space", None),
            P(None, "space", "member"),
        ),
        out_specs=(
            P("member", "space", None),
            P("member", "space", None),
            P(None, "member", "space"),
            P("member", None),
        ),
        check_vma=False,
    )
```

```python
import functools

import jax
import jax.numpy as jnp
import numpy as np
from jax import lax
from jax.experimental import pallas as pl
from jax.experimental.pallas import tpu as pltpu
from jax.sharding import PartitionSpec as P

MESH = pl.DeviceIdType.MESH
HIGHEST = lax.Precision.HIGHEST

time_step = 2e-05
alpha_coef = -5.0 / 9.0
beta_coef = 15.0 / 16.0
lorentz_rate = 25.0
wave_step = 0.5

CH = 96
LANES = 128
SLOT = 40


def cheb_matrix(points):
    intervals = points - 1
    index = np.arange(points)
    nodes = np.cos(np.pi * index / intervals)
    signs = np.ones(points)
    signs[0] = 2.0
    signs[-1] = 2.0
    signs = signs * (-1.0) ** index
    spread = nodes[:, None] - nodes[None, :]
    matrix = signs[:, None] / signs[None, :] / (spread + np.eye(points))
    matrix = matrix - np.eye(points) * matrix.sum(axis=1)[:, None]
    return matrix


def quad_weights(points):
    index = np.arange(points)
    return np.pi / (points - 1) * np.sin(np.pi * index / (points - 1))


def constants(space, members):
    points = 4 * space
    diff = cheb_matrix(points).astype(np.float32)
    both = np.stack([np.eye(points, dtype=np.float32), diff]).reshape(2, space, 4, points)
    both = both.transpose(1, 0, 2, 3).reshape(2 * points, points)
    weight = quad_weights(points)
    root = np.sqrt(np.maximum(weight, 0.0))
    lane_w = np.zeros((members, 16, LANES), np.float32)
    lane_w[:, :9] = np.repeat(root, CH).reshape(members, 9, LANES)
    z_w = np.zeros((space, 8, LANES), np.float32)
    z_w[:, :4] = root.reshape(space, 4, 1)
    return both, diff, lane_w, z_w


def mm(a, b, transpose_b=False):
    dims = (((1,), (1 if transpose_b else 0,)), ((), ()))
    return lax.dot_general(a, b, dims, precision=HIGHEST, preferred_element_type=jnp.float32)


def split(x):
    hi = x.astype(jnp.bfloat16)
    rest = x - hi.astype(jnp.float32)
    mid = rest.astype(jnp.bfloat16)
    lo = (rest - mid.astype(jnp.float32)).astype(jnp.bfloat16)
    return hi, mid, lo


def mm_exact(parts, b):
    dot = lambda a: jnp.dot(a, b, preferred_element_type=jnp.float32)
    return (dot(parts[2]) + dot(parts[1])) + dot(parts[0])


def iota(shape, axis):
    return lax.broadcasted_iota(jnp.int32, shape, axis)


def kernel(
    S,
    M,
    p_hbm,
    reg_hbm,
    v_hbm,
    a_hbm,
    dy_hbm,
    wl_hbm,
    wz_hbm,
    outf_ref,
    outa_ref,
    outr_ref,
    outg_ref,
    p_ref,
    reg_ref,
    v_ref,
    a_ref,
    dy_ref,
    wl_ref,
    wz_ref,
    sel_p,
    sel_d,
    send_b,
    recv_b,
    tpose,
    own_x,
    gath_x,
    xz,
    ct,
    send_c,
    recv_c,
    coef,
    sbuf,
    tbuf,
    rbuf,
    f_loc,
    a_loc,
    f_buf,
    g_buf,
    gp,
    gr,
    row,
    rows,
    send_sem,
    recv_sem,
    out_sem,
    in_sem,
):
    N = 4 * S
    H = S // 2
    m = lax.axis_index("member")
    s = lax.axis_index("space")

    def over_space(body):
        def step(k, carry):
            body(lax.rem(s + k, S))
            body(lax.rem(s + S - k, S))
            return carry

        lax.fori_loop(1, H, step, 0)
        body(lax.rem(s + H, S))

    def over_member(body):
        def step(k, carry):
            body(lax.rem(m + k, M))
            return carry

        lax.fori_loop(1, M, step, 0)

    def push(src, dst, which, member, space):
        pltpu.make_async_remote_copy(
            src_ref=src,
            dst_ref=dst,
            send_sem=send_sem.at[which],
            recv_sem=recv_sem.at[which],
            device_id=(member, space),
            device_id_type=MESH,
        ).start()

    def keep(src, dst, which):
        pltpu.make_async_copy(src, dst, recv_sem.at[which]).start()

    def arrived(ref, which):
        pltpu.make_async_copy(ref, ref, recv_sem.at[which]).wait()

    def sent(ref, which):
        pltpu.make_async_copy(ref, ref, send_sem.at[which]).wait()

    loads = [
        pltpu.make_async_copy(src, dst, in_sem.at[k])
        for k, (src, dst) in enumerate(
            (
                (v_hbm, v_ref),
                (p_hbm, p_ref),
                (a_hbm, a_ref),
                (dy_hbm, dy_ref),
                (reg_hbm, reg_ref),
                (wl_hbm.at[m], wl_ref),
                (wz_hbm.at[s], wz_ref),
            )
        )
    ]
    for load in loads:
        load.start()

    barrier = pltpu.get_barrier_semaphore()
    over_member(
        lambda t: pl.semaphore_signal(barrier, inc=1, device_id=(t, s), device_id_type=MESH)
    )
    over_space(
        lambda t: pl.semaphore_signal(barrier, inc=1, device_id=(m, t), device_id_type=MESH)
    )

    tpose[...] = jnp.zeros((LANES, LANES), jnp.float32)
    loads[0].wait()
    for c in range(3):
        tpose[4 * c : 4 * c + 4, 0:12] = v_ref[c]
    tpose[...] = tpose[...].T
    own_x[...] = (
        tpose[0:4, :]
        + pltpu.roll(tpose[4:8, :], 12, 1)
        + pltpu.roll(tpose[8:12, :], 24, 1)
    )
    loads[1].wait()
    loads[2].wait()
    send_b[...] = mm(a_ref[...], p_ref[...], transpose_b=True)
    group = iota((LANES, LANES), 0) // 4
    lane = iota((LANES, LANES), 1)
    comp = lane % 3
    kx = wave_step * (lane // 6 + 1).astype(jnp.float32)
    kx = jnp.where(lane % 6 < 3, kx, -kx)
    for z in range(4):
        chosen = [
            (group == 3 * z + 2).astype(jnp.float32),
            (group == 3 * z + 1).astype(jnp.float32),
            jnp.where(group == 3 * z, kx, 0.0),
            (group == 12 + 3 * z + comp).astype(jnp.float32),
        ]
        for k in range(4):
            sel_p[z, :, LANES * k : LANES * (k + 1)] = chosen[k].astype(jnp.bfloat16)
        sel_d[:, LANES * z : LANES * (z + 1)] = (
            (group == 3 * z + comp).astype(jnp.float32).astype(jnp.bfloat16)
        )
    for load in loads[3:]:
        load.wait()

    pl.semaphore_wait(barrier, S - 1 + M - 1)

    over_member(lambda t: push(own_x, gath_x.at[m], 0, t, s))
    keep(own_x, gath_x.at[m], 0)

    def bulk(first, last, which):
        mine = pl.ds(pl.multiple_of(8 * s, 8), 8)
        lanes = slice(first, last)

        def one(t):
            push(
                send_b.at[pl.ds(pl.multiple_of(8 * t, 8), 8), lanes],
                recv_b.at[mine, lanes],
                which,
                m,
                t,
            )

        over_space(one)
        keep(send_b.at[mine, lanes], recv_b.at[mine, lanes], which)

    bulk(0, 256, 1)

    arrived(gath_x, 0)
    for k in range(M):
        piece = gath_x[k]
        for j in range(3):
            part = piece if j == 0 else pltpu.roll(piece, LANES - 12 * j, 1)
            xz[12 * k + 4 * j : 12 * k + 4 * j + 4, :] = part
    x = jnp.where(iota((N, LANES), 1) < 12, xz[...], 0.0)
    ct[...] = mm(a_ref[...], x)
    packed = ct[pl.ds(0, S, stride=8), :]
    for k in range(1, 8):
        packed = packed + pltpu.roll(ct[pl.ds(k, S, stride=8), :], 12 * k, 1)
    send_c[:, 0, :] = packed
    over_space(lambda t: push(send_c.at[t], recv_c.at[s], 2, m, t))
    keep(send_c.at[s], recv_c.at[s], 2)
    bulk(256, 384, 6)

    arrived(recv_c, 2)
    spread = (iota((N, S), 0) // 4 == iota((N, S), 1)).astype(jnp.float32)
    wide = mm(spread, recv_c[:, 0, :])
    points = jnp.where(iota((N, LANES), 1) % 4 == iota((N, LANES), 0) % 4, wide, 0.0)
    dpoints = mm(dy_ref[...], points)
    parts = split(points)
    spread_y = mm_exact(split(dpoints), sel_d[...])
    for z in range(4):
        spread_p = mm_exact(parts, sel_p[z])
        for k in range(4):
            coef[k, z] = spread_p[:, LANES * k : LANES * (k + 1)]
        coef[4, z] = spread_y[:, LANES * z : LANES * (z + 1)]
    lane_n = iota((N, LANES), 1)
    lorentz = jnp.where(lane_n % 3 == 1, 0.0, lorentz_rate)

    pick = (iota((16, N), 1) == 12 * m + iota((16, N), 0)).astype(jnp.float32)

    def fold(x):
        x = x + pltpu.roll(x, LANES - 1, 1)
        return x + pltpu.roll(x, LANES - 2, 1)

    here = fold(mm(pick, points))
    there = fold(mm(pick, dpoints))
    which = (iota((16, LANES), 1) // 4) % 3
    back4 = pltpu.roll(here, LANES - 4, 1)
    back8 = pltpu.roll(here, LANES - 8, 1)
    on4 = pltpu.roll(here, 4, 1)
    vel_w = jnp.where(which == 0, back8, jnp.where(which == 1, back4, here))
    vel_v = jnp.where(which == 0, back4, jnp.where(which == 1, here, on4))
    drag = jnp.where(which == 1, 0.0, lorentz_rate)
    dz_here = pltpu.roll(here, LANES - 48, 1)
    tpose[...] = jnp.zeros((LANES, LANES), jnp.float32)
    tpose[0:16, :] = -vel_w * dz_here + (-vel_v * there - drag * here)
    tpose[...] = tpose[...].T
    y_row = 12 * m + iota((1, 12), 1)
    for z in range(4):
        z_row = 4 * s + z
        inside = (y_row > 0) & (y_row < N - 1) & (z_row > 0) & (z_row < N - 1)
        for c in range(3):
            at = 12 * z + 4 * c
            value = tpose[at : at + 1, 0:12]
            outr_ref[c, z : z + 1, :] = time_step * jnp.where(inside, value, 0.0)

    arrived(recv_b.at[:, 0:256], 1)
    arrived(recv_b.at[:, 256:384], 6)
    lane8 = iota((8, LANES), 1)

    def expand(step, carry):
        for u in range(3):
            r = 3 * step + u
            base = pl.ds(pl.multiple_of(8 * r, 8), 8)
            v0 = recv_b[base, 0:128]
            v1 = recv_b[base, 128:256]
            v2 = recv_b[base, 256:384]
            y1 = jnp.where(lane8 < 32, pltpu.roll(v0, 32, 1), pltpu.roll(v1, 32, 1))
            y2 = jnp.where(lane8 < 64, pltpu.roll(v1, 64, 1), pltpu.roll(v2, 64, 1))
            y3 = pltpu.roll(v2, 96, 1)
            for i, v in enumerate((v0, y1, y2, y3)):
                sbuf[pl.ds(pl.multiple_of(32 * r + 8 * i, 8), 8), :] = v
        return carry

    lax.fori_loop(0, S // 3, expand, 0)
    real = lane_n % 6 < 3
    comp_n = lane_n % 3
    half = N // 2
    for pair in range(2):
        q2 = jnp.concatenate(
            [sbuf[pl.ds(2 * pair + i, N, stride=8), :] for i in range(2)], axis=1
        )
        dyq2 = mm(dy_ref[...], q2)
        for i in range(2):
            z = 2 * pair + i
            q = q2[:, LANES * i : LANES * (i + 1)]
            dyq = dyq2[:, LANES * i : LANES * (i + 1)]
            dzq = sbuf[pl.ds(4 + z, N, stride=8), :]
            up1 = pltpu.roll(q, LANES - 1, 1)
            up2 = pltpu.roll(q, LANES - 2, 1)
            down1 = pltpu.roll(q, 1, 1)
            qz = jnp.where(comp_n == 0, up2, jnp.where(comp_n == 1, up1, q))
            qy = jnp.where(comp_n == 0, up1, jnp.where(comp_n == 1, q, down1))
            other = jnp.where(real, pltpu.roll(q, LANES - 3, 1), pltpu.roll(q, 3, 1))
            rhs = (-coef[0, z] * dzq - qz * coef[3, z]) + (
                -coef[1, z] * dyq + coef[2, z] * other - qy * coef[4, z] - lorentz * q
            )
            tbuf[pl.ds(z, half, stride=8), :] = rhs[0:half]
            tbuf[pl.ds(4 + z, half, stride=8), :] = rhs[half:N]

    def compact(step, carry):
        for u in range(3):
            r = 3 * step + u
            t = [tbuf[pl.ds(pl.multiple_of(32 * r + 8 * i, 8), 8), :] for i in range(4)]
            t1 = pltpu.roll(t[1], 96, 1)
            t2 = pltpu.roll(t[2], 64, 1)
            t3 = pltpu.roll(t[3], 32, 1)
            rbuf[r, :, 0:128] = jnp.where(lane8 < 96, t[0], t1)
            rbuf[r, :, 128:256] = jnp.where(lane8 < 64, t1, t2)
            rbuf[r, :, 256:384] = jnp.where(lane8 < 32, t2, t3)
        return carry

    lax.fori_loop(0, H // 3, compact, 0)
    z_rows = 4 * s + iota((4, 384), 0)
    z_mask = (z_rows > 0) & (z_rows < N - 1)
    lane_y = iota((4, 384), 1) // CH

    def slot_of(t):
        return pl.ds(pl.multiple_of(SLOT * t, 8), SLOT)

    def finish(g, carry):
        for h in range(2):
            slot = h * (S // 6) + g
            base = pl.multiple_of(SLOT * slot, 8)
            for i in range(3):
                r = h * H + 3 * g + i
                at = pl.ds(pl.multiple_of(384 * r, 128), 384)
                y = 4 * r + lane_y
                mask = jnp.where(z_mask & (y > 0) & (y < N - 1), 1.0, 0.0)
                rhs = rbuf[3 * g + i, 4 * h : 4 * h + 4, :]
                q = recv_b[pl.ds(pl.multiple_of(8 * r, 8), 4), :]
                acc = mask * (alpha_coef * reg_ref[:, at] + time_step * rhs)
                field = mask * (q + beta_coef * acc)
                a_loc[:, at] = acc
                f_loc[:, at] = field
                for l in range(3):
                    f_buf[pl.ds(base + 12 * i + 4 * l, 4), :] = field[:, 128 * l : 128 * l + 128]

            @pl.when(slot != m)
            def _():
                push(f_buf.at[slot_of(slot), :], g_buf.at[slot_of(m), :], 3, slot, s)

        return carry

    lax.fori_loop(0, S // 6, finish, 0)

    keep(f_buf.at[slot_of(m), :], g_buf.at[slot_of(m), :], 3)
    out_f = pltpu.make_async_copy(f_loc, outf_ref, out_sem.at[0])
    out_a = pltpu.make_async_copy(a_loc, outa_ref, out_sem.at[1])
    out_f.start()
    out_a.start()
    gp[...] = jnp.zeros((M, 1, LANES), jnp.float32)
    arrived(g_buf, 3)
    values = []
    for t in range(9):
        weight_y = wl_ref[t : t + 1, :]
        for z in range(4):
            value = g_buf[pl.ds(4 * t + z, M, stride=SLOT), :]
            values.append(split(value * (weight_y * wz_ref[z : z + 1, :])))
    stack = jnp.concatenate(
        [jnp.concatenate([v[k] for v in values], axis=1) for k in range(3)], axis=0
    )
    nine = lax.dot_general(
        stack, stack, (((1,), (1,)), ((), ())), preferred_element_type=jnp.float32
    )
    three = (nine[2 * M : 3 * M] + nine[M : 2 * M]) + nine[0:M]
    part = (three[:, 2 * M : 3 * M] + three[:, M : 2 * M]) + three[:, 0:M]
    for k in range(M):
        gp[k, :, 0:M] = part[k : k + 1, :]
    over_member(lambda t: push(gp.at[t], gr.at[m], 4, t, s))
    keep(gp.at[m], gr.at[m], 4)
    arrived(gr, 4)
    row[...] = jnp.sum(gr[...], axis=0)
    over_space(lambda t: push(row, rows.at[s], 5, m, t))
    keep(row, rows.at[s], 5)
    arrived(rows, 5)
    outg_ref[...] = (jnp.sum(rows[...], axis=0) / CH)[:, 0:M]

    sent(gath_x.at[0 : M - 1], 0)
    sent(recv_b.at[0 : 8 * (S - 1), 0:256], 1)
    sent(recv_b.at[0 : 8 * (S - 1), 256:384], 6)
    sent(recv_c.at[0 : S - 1], 2)
    sent(g_buf.at[0 : SLOT * (M - 1), :], 3)
    sent(gr.at[0 : M - 1], 4)
    sent(rows.at[0 : S - 1], 5)
    out_f.wait()
    out_a.wait()


def copy_kernel(*refs):
    n = (len(refs) - 2) // 3
    ins, outs, held = refs[:n], refs[n : 2 * n], refs[2 * n : 3 * n]
    in_sem, out_sem = refs[3 * n :]
    loads = [pltpu.make_async_copy(ins[k], held[k], in_sem.at[k]) for k in range(n)]
    stores = [pltpu.make_async_copy(held[k], outs[k], out_sem.at[k]) for k in range(n)]
    for load in loads:
        load.start()
    for load, store in zip(loads, stores):
        load.wait()
        store.start()
    for store in stores:
        store.wait()


def handed_on(arrays):
    hbm = pl.BlockSpec(memory_space=pl.ANY)
    n = len(arrays)
    return pl.pallas_call(
        copy_kernel,
        out_shape=[jax.ShapeDtypeStruct(a.shape, a.dtype) for a in arrays],
        in_specs=[hbm] * n,
        out_specs=[hbm] * n,
        scratch_shapes=[pltpu.VMEM(a.shape, a.dtype) for a in arrays]
        + [pltpu.SemaphoreType.DMA((n,)), pltpu.SemaphoreType.DMA((n,))],
        name="hand_on",
    )(*arrays)


def shards(S, M, perturb, register, ref_velocity):
    N = 4 * S
    f32 = jnp.float32
    both, diff, lane_w, z_w = constants(S, M)
    vmem = pl.BlockSpec(memory_space=pltpu.VMEM)
    hbm = pl.BlockSpec(memory_space=pl.ANY)
    outs = pl.pallas_call(
        functools.partial(kernel, S, M),
        out_shape=(
            jax.ShapeDtypeStruct((4, N * CH), f32),
            jax.ShapeDtypeStruct((4, N * CH), f32),
            jax.ShapeDtypeStruct((3, 4, 12), f32),
            jax.ShapeDtypeStruct((1, M), f32),
        ),
        in_specs=[hbm] * 7,
        out_specs=(hbm, hbm, vmem, vmem),
        scratch_shapes=[
            pltpu.VMEM((4 * CH, N), f32),
            pltpu.VMEM((4, N * CH), f32),
            pltpu.VMEM((3, 4, 12), f32),
            pltpu.VMEM((2 * N, N), f32),
            pltpu.VMEM((N, N), f32),
            pltpu.VMEM((16, LANES), f32),
            pltpu.VMEM((8, LANES), f32),
            pltpu.VMEM((4, LANES, 4 * LANES), jnp.bfloat16),
            pltpu.VMEM((LANES, 4 * LANES), jnp.bfloat16),
            pltpu.VMEM((2 * N, 384), f32),
            pltpu.VMEM((2 * N, 384), f32),
            pltpu.VMEM((LANES, LANES), f32),
            pltpu.VMEM((4, LANES), f32),
            pltpu.VMEM((M, 4, LANES), f32),
            pltpu.VMEM((N, LANES), f32),
            pltpu.VMEM((2 * N, LANES), f32),
            pltpu.VMEM((S, 1, LANES), f32),
            pltpu.VMEM((S, 1, LANES), f32),
            pltpu.VMEM((5, 4, N, LANES), f32),
            pltpu.VMEM((8 * N, LANES), f32),
            pltpu.VMEM((4 * N, LANES), f32),
            pltpu.VMEM((S // 2, 8, 384), f32),
            pltpu.VMEM((4, N * CH), f32),
            pltpu.VMEM((4, N * CH), f32),
            pltpu.VMEM((SLOT * M, LANES), f32),
            pltpu.VMEM((SLOT * M, LANES), f32),
            pltpu.VMEM((M, 1, LANES), f32),
            pltpu.VMEM((M, 1, LANES), f32),
            pltpu.VMEM((1, LANES), f32),
            pltpu.VMEM((S, 1, LANES), f32),
            pltpu.SemaphoreType.DMA((7,)),
            pltpu.SemaphoreType.DMA((7,)),
            pltpu.SemaphoreType.DMA((2,)),
            pltpu.SemaphoreType.DMA((7,)),
        ],
        compiler_params=pltpu.CompilerParams(collective_id=0, has_side_effects=True),
        name="substep",
    )(
        perturb.reshape(4 * CH, N),
        register[0],
        ref_velocity,
        jnp.asarray(both),
        jnp.asarray(diff),
        jnp.asarray(lane_w),
        jnp.asarray(z_w),
    )
    fields, acc, ref_step, gram = handed_on(outs)
    return fields[None], acc[None], jnp.transpose(ref_step, (0, 2, 1)), gram


def solution(mesh):
    return jax.shard_map(
        functools.partial(shards, mesh.shape["space"], mesh.shape["member"]),
        mesh=mesh,
        in_specs=(
            P("member", "space", None, None),
            P("member", "space", None),
            P(None, "space", "member"),
        ),
        out_specs=(
            P("member", "space", None),
            P("member", "space", None),
            P(None, "member", "space"),
            P("member", None),
        ),
        check_vma=False,
    )
```

```python
import functools

import jax
import jax.numpy as jnp
import numpy as np
from jax import lax
from jax.experimental import pallas as pl
from jax.experimental.pallas import tpu as pltpu
from jax.sharding import PartitionSpec as P

MESH = pl.DeviceIdType.MESH
HIGHEST = lax.Precision.HIGHEST

time_step = 2e-05
alpha_coef = -5.0 / 9.0
beta_coef = 15.0 / 16.0
lorentz_rate = 25.0
wave_step = 0.5

CH = 96
LANES = 128
SLOT = 40
USED = 36


def cheb_matrix(points):
    intervals = points - 1
    index = np.arange(points)
    nodes = np.cos(np.pi * index / intervals)
    signs = np.ones(points)
    signs[0] = 2.0
    signs[-1] = 2.0
    signs = signs * (-1.0) ** index
    spread = nodes[:, None] - nodes[None, :]
    matrix = signs[:, None] / signs[None, :] / (spread + np.eye(points))
    matrix = matrix - np.eye(points) * matrix.sum(axis=1)[:, None]
    return matrix


def quad_weights(points):
    index = np.arange(points)
    return np.pi / (points - 1) * np.sin(np.pi * index / (points - 1))


def constants(space, members):
    points = 4 * space
    diff = cheb_matrix(points).astype(np.float32)
    both = np.stack([np.eye(points, dtype=np.float32), diff]).reshape(2, space, 4, points)
    both = both.transpose(1, 0, 2, 3).reshape(2 * points, points)
    weight = quad_weights(points)
    root = np.sqrt(np.maximum(weight, 0.0))
    lane_w = np.zeros((members, 16, LANES), np.float32)
    lane_w[:, :9] = np.repeat(root, CH).reshape(members, 9, LANES)
    z_w = np.zeros((space, 8, LANES), np.float32)
    z_w[:, :4] = root.reshape(space, 4, 1)
    return both, diff, lane_w, z_w


def mm(a, b, transpose_b=False):
    dims = (((1,), (1 if transpose_b else 0,)), ((), ()))
    return lax.dot_general(a, b, dims, precision=HIGHEST, preferred_element_type=jnp.float32)


def split(x):
    hi = x.astype(jnp.bfloat16)
    rest = x - hi.astype(jnp.float32)
    mid = rest.astype(jnp.bfloat16)
    lo = (rest - mid.astype(jnp.float32)).astype(jnp.bfloat16)
    return hi, mid, lo


def mm_exact(parts, b):
    dot = lambda a: jnp.dot(a, b, preferred_element_type=jnp.float32)
    return (dot(parts[2]) + dot(parts[1])) + dot(parts[0])


def iota(shape, axis):
    return lax.broadcasted_iota(jnp.int32, shape, axis)


def kernel(
    S,
    M,
    p_hbm,
    reg_hbm,
    v_hbm,
    a_hbm,
    dy_hbm,
    wl_hbm,
    wz_hbm,
    f_loc,
    a_loc,
    outr_ref,
    outg_ref,
    p_ref,
    reg_ref,
    v_ref,
    a_ref,
    dy_ref,
    wl_ref,
    wz_ref,
    sel_p,
    sel_d,
    send_b,
    recv_b,
    tpose,
    own_x,
    gath_x,
    xz,
    ct,
    send_c,
    recv_c,
    coef,
    sbuf,
    dyq_b,
    tbuf,
    rbuf,
    f_buf,
    g_buf,
    gp,
    gr,
    row,
    rows,
    send_sem,
    recv_sem,
    in_sem,
):
    N = 4 * S
    H = S // 2
    m = lax.axis_index("member")
    s = lax.axis_index("space")

    def over_space(body):
        def step(k, carry):
            body(lax.rem(s + k, S))
            body(lax.rem(s + S - k, S))
            return carry

        lax.fori_loop(1, H, step, 0)
        body(lax.rem(s + H, S))

    def over_member(body):
        def step(k, carry):
            body(lax.rem(m + k, M))
            return carry

        lax.fori_loop(1, M, step, 0)

    def push(src, dst, which, member, space):
        pltpu.make_async_remote_copy(
            src_ref=src,
            dst_ref=dst,
            send_sem=send_sem.at[which],
            recv_sem=recv_sem.at[which],
            device_id=(member, space),
            device_id_type=MESH,
        ).start()

    def keep(src, dst, which):
        pltpu.make_async_copy(src, dst, recv_sem.at[which]).start()

    def arrived(ref, which):
        pltpu.make_async_copy(ref, ref, recv_sem.at[which]).wait()

    def sent(ref, which):
        pltpu.make_async_copy(ref, ref, send_sem.at[which]).wait()

    loads = [
        pltpu.make_async_copy(src, dst, in_sem.at[k])
        for k, (src, dst) in enumerate(
            (
                (v_hbm, v_ref),
                (p_hbm, p_ref),
                (a_hbm, a_ref),
                (dy_hbm, dy_ref),
                (reg_hbm, reg_ref),
                (wl_hbm.at[m], wl_ref),
                (wz_hbm.at[s], wz_ref),
            )
        )
    ]
    for load in loads:
        load.start()

    barrier = pltpu.get_barrier_semaphore()
    over_member(
        lambda t: pl.semaphore_signal(barrier, inc=1, device_id=(t, s), device_id_type=MESH)
    )
    over_space(
        lambda t: pl.semaphore_signal(barrier, inc=1, device_id=(m, t), device_id_type=MESH)
    )

    tpose[...] = jnp.zeros((LANES, LANES), jnp.float32)
    loads[0].wait()
    for c in range(3):
        tpose[4 * c : 4 * c + 4, 0:12] = v_ref[c]
    tpose[...] = tpose[...].T
    own_x[...] = (
        tpose[0:4, :]
        + pltpu.roll(tpose[4:8, :], 12, 1)
        + pltpu.roll(tpose[8:12, :], 24, 1)
    )
    loads[1].wait()
    loads[2].wait()
    send_b[...] = mm(a_ref[...], p_ref[...], transpose_b=True)
    pl.semaphore_wait(barrier, S - 1 + M - 1)

    over_member(lambda t: push(own_x, gath_x.at[m], 0, t, s))
    keep(own_x, gath_x.at[m], 0)

    def bulk(first, last, which):
        mine = pl.ds(pl.multiple_of(8 * s, 8), 8)
        lanes = slice(first, last)

        def one(t):
            push(
                send_b.at[pl.ds(pl.multiple_of(8 * t, 8), 8), lanes],
                recv_b.at[mine, lanes],
                which,
                m,
                t,
            )

        over_space(one)
        keep(send_b.at[mine, lanes], recv_b.at[mine, lanes], which)

    bulk(0, 256, 1)

    group = iota((LANES, LANES), 0) // 4
    lane = iota((LANES, LANES), 1)
    comp = lane % 3
    kx = wave_step * (lane // 6 + 1).astype(jnp.float32)
    kx = jnp.where(lane % 6 < 3, kx, -kx)
    for z in range(4):
        chosen = [
            (group == 3 * z + 2).astype(jnp.float32),
            (group == 3 * z + 1).astype(jnp.float32),
            jnp.where(group == 3 * z, kx, 0.0),
            (group == 12 + 3 * z + comp).astype(jnp.float32),
        ]
        for k in range(4):
            sel_p[z, :, LANES * k : LANES * (k + 1)] = chosen[k].astype(jnp.bfloat16)
        sel_d[:, LANES * z : LANES * (z + 1)] = (
            (group == 3 * z + comp).astype(jnp.float32).astype(jnp.bfloat16)
        )
    for load in loads[3:]:
        load.wait()

    arrived(gath_x, 0)
    for k in range(M):
        piece = gath_x[k]
        for j in range(3):
            part = piece if j == 0 else pltpu.roll(piece, LANES - 12 * j, 1)
            xz[12 * k + 4 * j : 12 * k + 4 * j + 4, :] = part
    x = jnp.where(iota((N, LANES), 1) < 12, xz[...], 0.0)
    xz[...] = x
    ct[...] = mm(dy_ref[...], x)
    packed = xz[pl.ds(0, S, stride=4), :]
    for z in range(1, 4):
        packed = packed + pltpu.roll(xz[pl.ds(z, S, stride=4), :], 12 * z, 1)
    for z in range(4):
        packed = packed + pltpu.roll(ct[pl.ds(z, S, stride=4), :], 48 + 12 * z, 1)
    send_c[:, 0, :] = packed
    over_space(lambda t: push(send_c.at[t], recv_c.at[s], 2, m, t))
    keep(send_c.at[s], recv_c.at[s], 2)
    bulk(256, 384, 6)

    arrived(recv_b.at[:, 0:256], 1)
    arrived(recv_b.at[:, 256:384], 6)
    lane8 = iota((8, LANES), 1)

    def expand(step, carry):
        for u in range(3):
            r = 3 * step + u
            base = pl.ds(pl.multiple_of(8 * r, 8), 8)
            v0 = recv_b[base, 0:128]
            v1 = recv_b[base, 128:256]
            v2 = recv_b[base, 256:384]
            y1 = jnp.where(lane8 < 32, pltpu.roll(v0, 32, 1), pltpu.roll(v1, 32, 1))
            y2 = jnp.where(lane8 < 64, pltpu.roll(v1, 64, 1), pltpu.roll(v2, 64, 1))
            y3 = pltpu.roll(v2, 96, 1)
            for i, v in enumerate((v0, y1, y2, y3)):
                sbuf[pl.ds(pl.multiple_of(32 * r + 8 * i, 8), 8), :] = v
        return carry

    lax.fori_loop(0, S // 3, expand, 0)
    for pair in range(2):
        q2 = jnp.concatenate(
            [sbuf[pl.ds(2 * pair + i, N, stride=8), :] for i in range(2)], axis=1
        )
        dyq_b[pair] = mm(dy_ref[...], q2)

    arrived(recv_c, 2)
    lane_s = iota((S, LANES), 1) % 4
    for k in range(4):
        xz[pl.ds(k, S, stride=4), :] = jnp.where(lane_s == k, recv_c[:, 0, :], 0.0)
    points = xz[...]
    dpoints = mm(dy_ref[...], points)
    parts = split(points)
    spread_y = mm_exact(split(dpoints), sel_d[...])
    for z in range(4):
        spread_p = mm_exact(parts, sel_p[z])
        for k in range(4):
            coef[k, z] = spread_p[:, LANES * k : LANES * (k + 1)]
        coef[4, z] = spread_y[:, LANES * z : LANES * (z + 1)]

    lane_n = iota((N, LANES), 1)
    lorentz = jnp.where(lane_n % 3 == 1, 0.0, lorentz_rate)

    real = lane_n % 6 < 3
    comp_n = lane_n % 3
    half = N // 2
    for z in range(4):
        q = sbuf[pl.ds(z, N, stride=8), :]
        dzq = sbuf[pl.ds(4 + z, N, stride=8), :]
        dyq = dyq_b[z // 2, :, LANES * (z % 2) : LANES * (z % 2 + 1)]
        up1 = pltpu.roll(q, LANES - 1, 1)
        up2 = pltpu.roll(q, LANES - 2, 1)
        down1 = pltpu.roll(q, 1, 1)
        qz = jnp.where(comp_n == 0, up2, jnp.where(comp_n == 1, up1, q))
        qy = jnp.where(comp_n == 0, up1, jnp.where(comp_n == 1, q, down1))
        other = jnp.where(real, pltpu.roll(q, LANES - 3, 1), pltpu.roll(q, 3, 1))
        rhs = (-coef[0, z] * dzq - qz * coef[3, z]) + (
            -coef[1, z] * dyq + coef[2, z] * other - qy * coef[4, z] - lorentz * q
        )
        tbuf[pl.ds(z, half, stride=8), :] = rhs[0:half]
        tbuf[pl.ds(4 + z, half, stride=8), :] = rhs[half:N]

    def compact(step, carry):
        for u in range(3):
            r = 3 * step + u
            t = [tbuf[pl.ds(pl.multiple_of(32 * r + 8 * i, 8), 8), :] for i in range(4)]
            t1 = pltpu.roll(t[1], 96, 1)
            t2 = pltpu.roll(t[2], 64, 1)
            t3 = pltpu.roll(t[3], 32, 1)
            rbuf[r, :, 0:128] = jnp.where(lane8 < 96, t[0], t1)
            rbuf[r, :, 128:256] = jnp.where(lane8 < 64, t1, t2)
            rbuf[r, :, 256:384] = jnp.where(lane8 < 32, t2, t3)
        return carry

    lax.fori_loop(0, H // 3, compact, 0)
    z_rows = 4 * s + iota((4, 384), 0)
    z_mask = (z_rows > 0) & (z_rows < N - 1)
    lane_y = iota((4, 384), 1) // CH

    def slot_of(t):
        return pl.ds(pl.multiple_of(SLOT * t, 8), USED)

    def finish(g, carry):
        for h in range(2):
            slot = h * (S // 6) + g
            base = pl.multiple_of(SLOT * slot, 8)
            for i in range(3):
                r = h * H + 3 * g + i
                at = pl.ds(pl.multiple_of(384 * r, 128), 384)
                y = 4 * r + lane_y
                mask = jnp.where(z_mask & (y > 0) & (y < N - 1), 1.0, 0.0)
                rhs = rbuf[3 * g + i, 4 * h : 4 * h + 4, :]
                q = recv_b[pl.ds(pl.multiple_of(8 * r, 8), 4), :]
                acc = mask * (alpha_coef * reg_ref[:, at] + time_step * rhs)
                field = mask * (q + beta_coef * acc)
                a_loc[:, at] = acc
                f_loc[:, at] = field
                for l in range(3):
                    f_buf[pl.ds(base + 12 * i + 4 * l, 4), :] = field[:, 128 * l : 128 * l + 128]

            @pl.when(slot != m)
            def _():
                push(f_buf.at[slot_of(slot), :], g_buf.at[slot_of(m), :], 3, slot, s)

        return carry

    lax.fori_loop(0, S // 6, finish, 0)

    keep(f_buf.at[slot_of(m), :], g_buf.at[slot_of(m), :], 3)
    pick = (iota((16, N), 1) == 12 * m + iota((16, N), 0)).astype(jnp.float32)

    def fold(x):
        x = x + pltpu.roll(x, LANES - 1, 1)
        return x + pltpu.roll(x, LANES - 2, 1)

    here = fold(mm(pick, points))
    there = fold(mm(pick, dpoints))
    which = (iota((16, LANES), 1) // 4) % 3
    back4 = pltpu.roll(here, LANES - 4, 1)
    back8 = pltpu.roll(here, LANES - 8, 1)
    on4 = pltpu.roll(here, 4, 1)
    vel_w = jnp.where(which == 0, back8, jnp.where(which == 1, back4, here))
    vel_v = jnp.where(which == 0, back4, jnp.where(which == 1, here, on4))
    drag = jnp.where(which == 1, 0.0, lorentz_rate)
    dz_here = pltpu.roll(here, LANES - 48, 1)
    tpose[...] = jnp.zeros((LANES, LANES), jnp.float32)
    tpose[0:16, :] = -vel_w * dz_here + (-vel_v * there - drag * here)
    tpose[...] = tpose[...].T
    y_row = 12 * m + iota((1, 12), 1)
    for z in range(4):
        z_row = 4 * s + z
        inside = (y_row > 0) & (y_row < N - 1) & (z_row > 0) & (z_row < N - 1)
        for c in range(3):
            at = 12 * z + 4 * c
            value = tpose[at : at + 1, 0:12]
            outr_ref[c, z : z + 1, :] = time_step * jnp.where(inside, value, 0.0)

    gp[...] = jnp.zeros((M, 1, LANES), jnp.float32)
    arrived(g_buf.at[0 : USED * M, :], 3)
    values = []
    for t in range(9):
        weight_y = wl_ref[t : t + 1, :]
        for z in range(4):
            value = g_buf[pl.ds(4 * t + z, M, stride=SLOT), :]
            values.append(split(value * (weight_y * wz_ref[z : z + 1, :])))
    stack = jnp.concatenate(
        [jnp.concatenate([v[k] for v in values], axis=1) for k in range(3)], axis=0
    )
    nine = lax.dot_general(
        stack, stack, (((1,), (1,)), ((), ())), preferred_element_type=jnp.float32
    )
    three = (nine[2 * M : 3 * M] + nine[M : 2 * M]) + nine[0:M]
    part = (three[:, 2 * M : 3 * M] + three[:, M : 2 * M]) + three[:, 0:M]
    for k in range(M):
        gp[k, :, 0:M] = part[k : k + 1, :]
    over_member(lambda t: push(gp.at[t], gr.at[m], 4, t, s))
    keep(gp.at[m], gr.at[m], 4)
    arrived(gr, 4)
    row[...] = jnp.sum(gr[...], axis=0)
    over_space(lambda t: push(row, rows.at[s], 5, m, t))
    keep(row, rows.at[s], 5)
    arrived(rows, 5)
    outg_ref[...] = (jnp.sum(rows[...], axis=0) / CH)[:, 0:M]

    sent(gath_x.at[0 : M - 1], 0)
    sent(recv_b.at[0 : 8 * (S - 1), 0:256], 1)
    sent(recv_b.at[0 : 8 * (S - 1), 256:384], 6)
    sent(recv_c.at[0 : S - 1], 2)
    sent(g_buf.at[0 : USED * (M - 1), :], 3)
    sent(gr.at[0 : M - 1], 4)
    sent(rows.at[0 : S - 1], 5)


def copy_kernel(*refs):
    n = (len(refs) - 1) // 2
    stores = [pltpu.make_async_copy(refs[k], refs[n + k], refs[-1].at[k]) for k in range(n)]
    for store in stores:
        store.start()
    for store in stores:
        store.wait()


def handed_on(arrays):
    n = len(arrays)
    arrays = [pltpu.with_memory_space_constraint(a, pltpu.VMEM) for a in arrays]
    return pl.pallas_call(
        copy_kernel,
        out_shape=[jax.ShapeDtypeStruct(a.shape, a.dtype) for a in arrays],
        in_specs=[pl.BlockSpec(memory_space=pltpu.VMEM)] * n,
        out_specs=[pl.BlockSpec(memory_space=pl.ANY)] * n,
        scratch_shapes=[pltpu.SemaphoreType.DMA((n,))],
        name="hand_on",
    )(*arrays)


def shards(S, M, perturb, register, ref_velocity):
    N = 4 * S
    f32 = jnp.float32
    both, diff, lane_w, z_w = constants(S, M)
    vmem = pl.BlockSpec(memory_space=pltpu.VMEM)
    hbm = pl.BlockSpec(memory_space=pl.ANY)
    outs = pl.pallas_call(
        functools.partial(kernel, S, M),
        out_shape=(
            pltpu.VMEM((4, N * CH), f32),
            pltpu.VMEM((4, N * CH), f32),
            pltpu.VMEM((3, 4, 12), f32),
            pltpu.VMEM((1, M), f32),
        ),
        in_specs=[hbm] * 7,
        out_specs=(vmem,) * 4,
        scratch_shapes=[
            pltpu.VMEM((4 * CH, N), f32),
            pltpu.VMEM((4, N * CH), f32),
            pltpu.VMEM((3, 4, 12), f32),
            pltpu.VMEM((2 * N, N), f32),
            pltpu.VMEM((N, N), f32),
            pltpu.VMEM((16, LANES), f32),
            pltpu.VMEM((8, LANES), f32),
            pltpu.VMEM((4, LANES, 4 * LANES), jnp.bfloat16),
            pltpu.VMEM((LANES, 4 * LANES), jnp.bfloat16),
            pltpu.VMEM((2 * N, 384), f32),
            pltpu.VMEM((2 * N, 384), f32),
            pltpu.VMEM((LANES, LANES), f32),
            pltpu.VMEM((4, LANES), f32),
            pltpu.VMEM((M, 4, LANES), f32),
            pltpu.VMEM((N, LANES), f32),
            pltpu.VMEM((N, LANES), f32),
            pltpu.VMEM((S, 1, LANES), f32),
            pltpu.VMEM((S, 1, LANES), f32),
            pltpu.VMEM((5, 4, N, LANES), f32),
            pltpu.VMEM((8 * N, LANES), f32),
            pltpu.VMEM((2, N, 2 * LANES), f32),
            pltpu.VMEM((4 * N, LANES), f32),
            pltpu.VMEM((S // 2, 8, 384), f32),
            pltpu.VMEM((SLOT * M, LANES), f32),
            pltpu.VMEM((SLOT * M, LANES), f32),
            pltpu.VMEM((M, 1, LANES), f32),
            pltpu.VMEM((M, 1, LANES), f32),
            pltpu.VMEM((1, LANES), f32),
            pltpu.VMEM((S, 1, LANES), f32),
            pltpu.SemaphoreType.DMA((7,)),
            pltpu.SemaphoreType.DMA((7,)),
            pltpu.SemaphoreType.DMA((7,)),
        ],
        compiler_params=pltpu.CompilerParams(collective_id=0, has_side_effects=True),
        name="substep",
    )(
        perturb.reshape(4 * CH, N),
        register[0],
        ref_velocity,
        jnp.asarray(both),
        jnp.asarray(diff),
        jnp.asarray(lane_w),
        jnp.asarray(z_w),
    )
    fields, acc, ref_step, gram = handed_on(outs)
    return fields[None], acc[None], jnp.transpose(ref_step, (0, 2, 1)), gram


def solution(mesh):
    return jax.shard_map(
        functools.partial(shards, mesh.shape["space"], mesh.shape["member"]),
        mesh=mesh,
        in_specs=(
            P("member", "space", None, None),
            P("member", "space", None),
            P(None, "space", "member"),
        ),
        out_specs=(
            P("member", "space", None),
            P("member", "space", None),
            P(None, "member", "space"),
            P("member", None),
        ),
        check_vma=False,
    )
```

```python
import functools

import jax
import jax.numpy as jnp
import numpy as np
from jax import lax
from jax.experimental import pallas as pl
from jax.experimental.pallas import tpu as pltpu
from jax.sharding import PartitionSpec as P

MESH = pl.DeviceIdType.MESH
HIGHEST = lax.Precision.HIGHEST

time_step = 2e-05
alpha_coef = -5.0 / 9.0
beta_coef = 15.0 / 16.0
lorentz_rate = 25.0
wave_step = 0.5

CH = 96
LANES = 128
SLOT = 40
USED = 36
EXPAND = 6


def cheb_matrix(points):
    intervals = points - 1
    index = np.arange(points)
    nodes = np.cos(np.pi * index / intervals)
    signs = np.ones(points)
    signs[0] = 2.0
    signs[-1] = 2.0
    signs = signs * (-1.0) ** index
    spread = nodes[:, None] - nodes[None, :]
    matrix = signs[:, None] / signs[None, :] / (spread + np.eye(points))
    matrix = matrix - np.eye(points) * matrix.sum(axis=1)[:, None]
    return matrix


def quad_weights(points):
    index = np.arange(points)
    return np.pi / (points - 1) * np.sin(np.pi * index / (points - 1))


def parts_of(matrix):
    hi = matrix.astype(jnp.bfloat16)
    mid = (matrix - hi.astype(np.float32)).astype(jnp.bfloat16)
    return np.stack([hi, mid])


def constants(space, members):
    points = 4 * space
    diff = cheb_matrix(points).astype(np.float32)
    both = np.stack([np.eye(points, dtype=np.float32), diff]).reshape(2, space, 4, points)
    both = both.transpose(1, 0, 2, 3).reshape(2 * points, points)
    weight = quad_weights(points)
    root = np.sqrt(np.maximum(weight, 0.0))
    lane_w = np.zeros((members, 16, LANES), np.float32)
    lane_w[:, :9] = np.repeat(root, CH).reshape(members, 9, LANES)
    z_w = np.zeros((space, 8, LANES), np.float32)
    z_w[:, :4] = root.reshape(space, 4, 1)
    return parts_of(both), diff, parts_of(diff), lane_w, z_w


def mm(a, b, transpose_b=False):
    dims = (((1,), (1 if transpose_b else 0,)), ((), ()))
    return lax.dot_general(a, b, dims, precision=HIGHEST, preferred_element_type=jnp.float32)


def split(x):
    hi = x.astype(jnp.bfloat16)
    rest = x - hi.astype(jnp.float32)
    mid = rest.astype(jnp.bfloat16)
    lo = (rest - mid.astype(jnp.float32)).astype(jnp.bfloat16)
    return hi, mid, lo


def mm_bf(a, b, contract_b=0):
    dims = (((1,), (contract_b,)), ((), ()))
    return lax.dot_general(a, b, dims, preferred_element_type=jnp.float32)


def mm_exact(parts, b):
    return (mm_bf(parts[2], b) + mm_bf(parts[1], b)) + mm_bf(parts[0], b)


def iota(shape, axis):
    return lax.broadcasted_iota(jnp.int32, shape, axis)


def kernel(
    S,
    M,
    p_hbm,
    reg_hbm,
    v_hbm,
    a_hbm,
    dy_hbm,
    dp_hbm,
    wl_hbm,
    wz_hbm,
    f_loc,
    a_loc,
    outr_ref,
    outg_ref,
    p_ref,
    reg_ref,
    v_ref,
    a_ref,
    dy_ref,
    dp_ref,
    wl_ref,
    wz_ref,
    sel_p,
    sel_d,
    send_b,
    recv_b,
    tpose,
    own_x,
    gath_x,
    xz,
    ct,
    send_c,
    recv_c,
    coef,
    sbuf,
    dyq_b,
    tbuf,
    rbuf,
    f_buf,
    g_buf,
    gp,
    gr,
    row,
    rows,
    send_sem,
    recv_sem,
    in_sem,
):
    N = 4 * S
    H = S // 2
    m = lax.axis_index("member")
    s = lax.axis_index("space")

    def wrap(value, size):
        return jnp.where(value >= size, value - size, value)

    def over_space(body):
        def step(k, carry):
            body(wrap(s + k, S))
            body(wrap(s + S - k, S))
            return carry

        lax.fori_loop(1, H, step, 0)
        body(wrap(s + H, S))

    def each_space(body):
        for k in range(1, H):
            body(wrap(s + k, S))
            body(wrap(s + S - k, S))
        body(wrap(s + H, S))

    def over_member(body):
        for k in range(1, M):
            body(wrap(m + k, M))

    def push(src, dst, which, member, space):
        pltpu.make_async_remote_copy(
            src_ref=src,
            dst_ref=dst,
            send_sem=send_sem.at[which],
            recv_sem=recv_sem.at[which],
            device_id=(member, space),
            device_id_type=MESH,
        ).start()

    def keep(src, dst, which):
        pltpu.make_async_copy(src, dst, recv_sem.at[which]).start()

    def arrived(ref, which):
        pltpu.make_async_copy(ref, ref, recv_sem.at[which]).wait()

    def sent(ref, which):
        pltpu.make_async_copy(ref, ref, send_sem.at[which]).wait()

    loads = [
        pltpu.make_async_copy(src, dst, in_sem.at[k])
        for k, (src, dst) in enumerate(
            (
                (v_hbm, v_ref),
                (p_hbm, p_ref),
                (a_hbm, a_ref),
                (dy_hbm, dy_ref),
                (dp_hbm, dp_ref),
                (reg_hbm, reg_ref),
                (wl_hbm.at[m], wl_ref),
                (wz_hbm.at[s], wz_ref),
            )
        )
    ]
    for load in loads:
        load.start()

    barrier = pltpu.get_barrier_semaphore()
    over_member(
        lambda t: pl.semaphore_signal(barrier, inc=1, device_id=(t, s), device_id_type=MESH)
    )
    each_space(
        lambda t: pl.semaphore_signal(barrier, inc=1, device_id=(m, t), device_id_type=MESH)
    )

    tpose[...] = jnp.zeros((LANES, LANES), jnp.float32)
    loads[0].wait()
    for c in range(3):
        tpose[4 * c : 4 * c + 4, 0:12] = v_ref[c]
    tpose[...] = tpose[...].T
    own_x[...] = (
        tpose[0:4, :]
        + pltpu.roll(tpose[4:8, :], 12, 1)
        + pltpu.roll(tpose[8:12, :], 24, 1)
    )
    loads[1].wait()
    loads[2].wait()
    q_hi, q_mid, q_lo = split(p_ref[...])
    send_b[...] = (
        (mm_bf(a_ref[0], q_lo, 1) + mm_bf(a_ref[1], q_hi, 1)) + mm_bf(a_ref[0], q_mid, 1)
    ) + mm_bf(a_ref[0], q_hi, 1)
    pl.semaphore_wait(barrier, S - 1 + M - 1)

    over_member(lambda t: push(own_x, gath_x.at[m], 0, t, s))
    keep(own_x, gath_x.at[m], 0)

    def bulk(first, last, which):
        mine = pl.ds(pl.multiple_of(8 * s, 8), 8)
        lanes = slice(first, last)

        def one(t):
            push(
                send_b.at[pl.ds(pl.multiple_of(8 * t, 8), 8), lanes],
                recv_b.at[mine, lanes],
                which,
                m,
                t,
            )

        over_space(one)
        keep(send_b.at[mine, lanes], recv_b.at[mine, lanes], which)

    bulk(0, 256, 1)

    group = iota((LANES, LANES), 0) // 4
    lane = iota((LANES, LANES), 1)
    comp = lane % 3
    kx = wave_step * (lane // 6 + 1).astype(jnp.float32)
    kx = jnp.where(lane % 6 < 3, kx, -kx)
    for z in range(4):
        chosen = [
            (group == 3 * z + 2).astype(jnp.float32),
            (group == 3 * z + 1).astype(jnp.float32),
            jnp.where(group == 3 * z, kx, 0.0),
            (group == 12 + 3 * z + comp).astype(jnp.float32),
        ]
        for k in range(4):
            sel_p[z, :, LANES * k : LANES * (k + 1)] = chosen[k].astype(jnp.bfloat16)
        sel_d[:, LANES * z : LANES * (z + 1)] = (
            (group == 3 * z + comp).astype(jnp.float32).astype(jnp.bfloat16)
        )
    for load in loads[3:]:
        load.wait()

    arrived(gath_x, 0)
    for k in range(M):
        piece = gath_x[k]
        for j in range(3):
            part = piece if j == 0 else pltpu.roll(piece, LANES - 12 * j, 1)
            xz[12 * k + 4 * j : 12 * k + 4 * j + 4, :] = part
    x = jnp.where(iota((N, LANES), 1) < 12, xz[...], 0.0)
    xz[...] = x
    ct[...] = mm(dy_ref[...], x)
    packed = xz[pl.ds(0, S, stride=4), :]
    for z in range(1, 4):
        packed = packed + pltpu.roll(xz[pl.ds(z, S, stride=4), :], 12 * z, 1)
    for z in range(4):
        packed = packed + pltpu.roll(ct[pl.ds(z, S, stride=4), :], 48 + 12 * z, 1)
    send_c[:, 0, :] = packed
    over_space(lambda t: push(send_c.at[t], recv_c.at[s], 2, m, t))
    keep(send_c.at[s], recv_c.at[s], 2)
    bulk(256, 384, 6)

    lane8 = iota((8, LANES), 1)

    def expand(last):
        def go(step, carry):
            for u in range(EXPAND):
                r = EXPAND * step + u
                base = pl.ds(pl.multiple_of(8 * r, 8), 8)
                v1 = recv_b[base, 128:256]
                if last:
                    v2 = recv_b[base, 256:384]
                    tiles = (
                        jnp.where(lane8 < 64, pltpu.roll(v1, 64, 1), pltpu.roll(v2, 64, 1)),
                        pltpu.roll(v2, 96, 1),
                    )
                else:
                    v0 = recv_b[base, 0:128]
                    tiles = (
                        v0,
                        jnp.where(lane8 < 32, pltpu.roll(v0, 32, 1), pltpu.roll(v1, 32, 1)),
                    )
                for i, v in enumerate(tiles):
                    at = 32 * r + 8 * (i + 2 * last)
                    sbuf[pl.ds(pl.multiple_of(at, 8), 8), :] = v
            return carry

        lax.fori_loop(0, S // EXPAND, go, 0)

    arrived(recv_b.at[:, 0:256], 1)
    expand(0)

    arrived(recv_c, 2)
    lane_s = iota((S, LANES), 1) % 4
    for k in range(4):
        xz[pl.ds(k, S, stride=4), :] = jnp.where(lane_s == k, recv_c[:, 0, :], 0.0)
    points = xz[...]
    dpoints = mm(dy_ref[...], points)
    parts = split(points)
    spread_y = mm_exact(split(dpoints), sel_d[...])
    for z in range(4):
        spread_p = mm_exact(parts, sel_p[z])
        for k in range(4):
            coef[k, z] = spread_p[:, LANES * k : LANES * (k + 1)]
        coef[4, z] = spread_y[:, LANES * z : LANES * (z + 1)]


    arrived(recv_b.at[:, 256:384], 6)
    expand(1)
    for pair in range(2):
        q2 = jnp.concatenate(
            [sbuf[pl.ds(2 * pair + i, N, stride=8), :] for i in range(2)], axis=1
        )
        q_hi, q_mid, _ = split(q2)
        dyq_b[pair] = (mm_bf(dp_ref[0], q_mid) + mm_bf(dp_ref[1], q_hi)) + mm_bf(dp_ref[0], q_hi)

    lane_n = iota((N, LANES), 1)
    lorentz = jnp.where(lane_n % 3 == 1, 0.0, lorentz_rate)

    real = lane_n % 6 < 3
    comp_n = lane_n % 3
    half = N // 2
    for z in range(4):
        q = sbuf[pl.ds(z, N, stride=8), :]
        dzq = sbuf[pl.ds(4 + z, N, stride=8), :]
        dyq = dyq_b[z // 2, :, LANES * (z % 2) : LANES * (z % 2 + 1)]
        up1 = pltpu.roll(q, LANES - 1, 1)
        up2 = pltpu.roll(q, LANES - 2, 1)
        down1 = pltpu.roll(q, 1, 1)
        qz = jnp.where(comp_n == 0, up2, jnp.where(comp_n == 1, up1, q))
        qy = jnp.where(comp_n == 0, up1, jnp.where(comp_n == 1, q, down1))
        other = jnp.where(real, pltpu.roll(q, LANES - 3, 1), pltpu.roll(q, 3, 1))
        rhs = (-coef[0, z] * dzq - qz * coef[3, z]) + (
            -coef[1, z] * dyq + coef[2, z] * other - qy * coef[4, z] - lorentz * q
        )
        tbuf[pl.ds(z, half, stride=8), :] = rhs[0:half]
        tbuf[pl.ds(4 + z, half, stride=8), :] = rhs[half:N]

    def compact(step, carry):
        for u in range(3):
            r = 3 * step + u
            t = [tbuf[pl.ds(pl.multiple_of(32 * r + 8 * i, 8), 8), :] for i in range(4)]
            t1 = pltpu.roll(t[1], 96, 1)
            t2 = pltpu.roll(t[2], 64, 1)
            t3 = pltpu.roll(t[3], 32, 1)
            rbuf[r, :, 0:128] = jnp.where(lane8 < 96, t[0], t1)
            rbuf[r, :, 128:256] = jnp.where(lane8 < 64, t1, t2)
            rbuf[r, :, 256:384] = jnp.where(lane8 < 32, t2, t3)
        return carry

    lax.fori_loop(0, H // 3, compact, 0)
    z_rows = 4 * s + iota((4, 384), 0)
    z_mask = (z_rows > 0) & (z_rows < N - 1)
    lane_y = iota((4, 384), 1) // CH

    def slot_of(t):
        return pl.ds(pl.multiple_of(SLOT * t, 8), USED)

    def finish(step, carry):
        g = lax.rem(m + 1 + step, S // 6)
        for h in range(2):
            slot = h * (S // 6) + g
            base = pl.multiple_of(SLOT * slot, 8)
            for i in range(3):
                r = h * H + 3 * g + i
                at = pl.ds(pl.multiple_of(384 * r, 128), 384)
                y = 4 * r + lane_y
                mask = jnp.where(z_mask & (y > 0) & (y < N - 1), 1.0, 0.0)
                rhs = rbuf[3 * g + i, 4 * h : 4 * h + 4, :]
                q = recv_b[pl.ds(pl.multiple_of(8 * r, 8), 4), :]
                acc = mask * (alpha_coef * reg_ref[:, at] + time_step * rhs)
                field = mask * (q + beta_coef * acc)
                a_loc[:, at] = acc
                f_loc[:, at] = field
                for l in range(3):
                    f_buf[pl.ds(base + 12 * i + 4 * l, 4), :] = field[:, 128 * l : 128 * l + 128]

            @pl.when(slot != m)
            def _():
                push(f_buf.at[slot_of(slot), :], g_buf.at[slot_of(m), :], 3, slot, s)

        return carry

    lax.fori_loop(0, S // 6, finish, 0)

    keep(f_buf.at[slot_of(m), :], g_buf.at[slot_of(m), :], 3)
    pick = (iota((16, N), 1) == 12 * m + iota((16, N), 0)).astype(jnp.float32)

    def fold(x):
        x = x + pltpu.roll(x, LANES - 1, 1)
        return x + pltpu.roll(x, LANES - 2, 1)

    here = fold(mm(pick, points))
    there = fold(mm(pick, dpoints))
    which = (iota((16, LANES), 1) // 4) % 3
    back4 = pltpu.roll(here, LANES - 4, 1)
    back8 = pltpu.roll(here, LANES - 8, 1)
    on4 = pltpu.roll(here, 4, 1)
    vel_w = jnp.where(which == 0, back8, jnp.where(which == 1, back4, here))
    vel_v = jnp.where(which == 0, back4, jnp.where(which == 1, here, on4))
    drag = jnp.where(which == 1, 0.0, lorentz_rate)
    dz_here = pltpu.roll(here, LANES - 48, 1)
    tpose[...] = jnp.zeros((LANES, LANES), jnp.float32)
    tpose[0:16, :] = -vel_w * dz_here + (-vel_v * there - drag * here)
    tpose[...] = tpose[...].T
    y_row = 12 * m + iota((1, 12), 1)
    for z in range(4):
        z_row = 4 * s + z
        inside = (y_row > 0) & (y_row < N - 1) & (z_row > 0) & (z_row < N - 1)
        for c in range(3):
            at = 12 * z + 4 * c
            value = tpose[at : at + 1, 0:12]
            outr_ref[c, z : z + 1, :] = time_step * jnp.where(inside, value, 0.0)

    gp[...] = jnp.zeros((M, 1, LANES), jnp.float32)
    arrived(g_buf.at[0 : USED * M, :], 3)
    values = []
    for t in range(9):
        weight_y = wl_ref[t : t + 1, :]
        for z in range(4):
            value = g_buf[pl.ds(4 * t + z, M, stride=SLOT), :]
            values.append(split(value * (weight_y * wz_ref[z : z + 1, :])))
    stack = jnp.concatenate(
        [jnp.concatenate([v[k] for v in values], axis=1) for k in range(3)], axis=0
    )
    nine = lax.dot_general(
        stack, stack, (((1,), (1,)), ((), ())), preferred_element_type=jnp.float32
    )
    three = (nine[2 * M : 3 * M] + nine[M : 2 * M]) + nine[0:M]
    part = (three[:, 2 * M : 3 * M] + three[:, M : 2 * M]) + three[:, 0:M]
    for k in range(M):
        gp[k, :, 0:M] = part[k : k + 1, :]
    over_member(lambda t: push(gp.at[t], gr.at[m], 4, t, s))
    keep(gp.at[m], gr.at[m], 4)
    arrived(gr, 4)
    row[...] = jnp.sum(gr[...], axis=0)
    each_space(lambda t: push(row, rows.at[s], 5, m, t))
    keep(row, rows.at[s], 5)
    arrived(rows, 5)
    outg_ref[...] = (jnp.sum(rows[...], axis=0) / CH)[:, 0:M]

    sent(gath_x.at[0 : M - 1], 0)
    sent(recv_b.at[0 : 8 * (S - 1), 0:256], 1)
    sent(recv_b.at[0 : 8 * (S - 1), 256:384], 6)
    sent(recv_c.at[0 : S - 1], 2)
    sent(g_buf.at[0 : USED * (M - 1), :], 3)
    sent(gr.at[0 : M - 1], 4)
    sent(rows.at[0 : S - 1], 5)


def copy_kernel(*refs):
    n = (len(refs) - 1) // 2
    stores = [pltpu.make_async_copy(refs[k], refs[n + k], refs[-1].at[k]) for k in range(n)]
    for store in stores:
        store.start()
    for store in stores:
        store.wait()


def handed_on(arrays):
    n = len(arrays)
    arrays = [pltpu.with_memory_space_constraint(a, pltpu.VMEM) for a in arrays]
    return pl.pallas_call(
        copy_kernel,
        out_shape=[jax.ShapeDtypeStruct(a.shape, a.dtype) for a in arrays],
        in_specs=[pl.BlockSpec(memory_space=pltpu.VMEM)] * n,
        out_specs=[pl.BlockSpec(memory_space=pl.ANY)] * n,
        scratch_shapes=[pltpu.SemaphoreType.DMA((n,))],
        name="hand_on",
    )(*arrays)


def shards(S, M, perturb, register, ref_velocity):
    N = 4 * S
    f32 = jnp.float32
    both, diff, diff_parts, lane_w, z_w = constants(S, M)
    vmem = pl.BlockSpec(memory_space=pltpu.VMEM)
    hbm = pl.BlockSpec(memory_space=pl.ANY)
    outs = pl.pallas_call(
        functools.partial(kernel, S, M),
        out_shape=(
            pltpu.VMEM((4, N * CH), f32),
            pltpu.VMEM((4, N * CH), f32),
            pltpu.VMEM((3, 4, 12), f32),
            pltpu.VMEM((1, M), f32),
        ),
        in_specs=[hbm] * 8,
        out_specs=(vmem,) * 4,
        scratch_shapes=[
            pltpu.VMEM((4 * CH, N), f32),
            pltpu.VMEM((4, N * CH), f32),
            pltpu.VMEM((3, 4, 12), f32),
            pltpu.VMEM((2, 2 * N, N), jnp.bfloat16),
            pltpu.VMEM((N, N), f32),
            pltpu.VMEM((2, N, N), jnp.bfloat16),
            pltpu.VMEM((16, LANES), f32),
            pltpu.VMEM((8, LANES), f32),
            pltpu.VMEM((4, LANES, 4 * LANES), jnp.bfloat16),
            pltpu.VMEM((LANES, 4 * LANES), jnp.bfloat16),
            pltpu.VMEM((2 * N, 384), f32),
            pltpu.VMEM((2 * N, 384), f32),
            pltpu.VMEM((LANES, LANES), f32),
            pltpu.VMEM((4, LANES), f32),
            pltpu.VMEM((M, 4, LANES), f32),
            pltpu.VMEM((N, LANES), f32),
            pltpu.VMEM((N, LANES), f32),
            pltpu.VMEM((S, 1, LANES), f32),
            pltpu.VMEM((S, 1, LANES), f32),
            pltpu.VMEM((5, 4, N, LANES), f32),
            pltpu.VMEM((8 * N, LANES), f32),
            pltpu.VMEM((2, N, 2 * LANES), f32),
            pltpu.VMEM((4 * N, LANES), f32),
            pltpu.VMEM((S // 2, 8, 384), f32),
            pltpu.VMEM((SLOT * M, LANES), f32),
            pltpu.VMEM((SLOT * M, LANES), f32),
            pltpu.VMEM((M, 1, LANES), f32),
            pltpu.VMEM((M, 1, LANES), f32),
            pltpu.VMEM((1, LANES), f32),
            pltpu.VMEM((S, 1, LANES), f32),
            pltpu.SemaphoreType.DMA((7,)),
            pltpu.SemaphoreType.DMA((7,)),
            pltpu.SemaphoreType.DMA((8,)),
        ],
        compiler_params=pltpu.CompilerParams(collective_id=0, has_side_effects=True),
        name="substep",
    )(
        perturb.reshape(4 * CH, N),
        register[0],
        ref_velocity,
        jnp.asarray(both),
        jnp.asarray(diff),
        jnp.asarray(diff_parts),
        jnp.asarray(lane_w),
        jnp.asarray(z_w),
    )
    fields, acc, ref_step, gram = handed_on(outs)
    return fields[None], acc[None], jnp.transpose(ref_step, (0, 2, 1)), gram


def solution(mesh):
    return jax.shard_map(
        functools.partial(shards, mesh.shape["space"], mesh.shape["member"]),
        mesh=mesh,
        in_specs=(
            P("member", "space", None, None),
            P("member", "space", None),
            P(None, "space", "member"),
        ),
        out_specs=(
            P("member", "space", None),
            P("member", "space", None),
            P(None, "member", "space"),
            P("member", None),
        ),
        check_vma=False,
    )
```

```python
import functools

import jax
import jax.numpy as jnp
import numpy as np
from jax import lax
from jax.experimental import pallas as pl
from jax.experimental.pallas import tpu as pltpu
from jax.sharding import PartitionSpec as P

MESH = pl.DeviceIdType.MESH
HIGHEST = lax.Precision.HIGHEST

time_step = 2e-05
alpha_coef = -5.0 / 9.0
beta_coef = 15.0 / 16.0
lorentz_rate = 25.0
wave_step = 0.5

CH = 96
LANES = 128
SLOT = 40
USED = 36
EXPAND = 6
FAR = {8: (4, 3, 5, 2, 6, 1, 7, 0), 1: (0,)}


def cheb_matrix(points):
    intervals = points - 1
    index = np.arange(points)
    nodes = np.cos(np.pi * index / intervals)
    signs = np.ones(points)
    signs[0] = 2.0
    signs[-1] = 2.0
    signs = signs * (-1.0) ** index
    spread = nodes[:, None] - nodes[None, :]
    matrix = signs[:, None] / signs[None, :] / (spread + np.eye(points))
    matrix = matrix - np.eye(points) * matrix.sum(axis=1)[:, None]
    return matrix


def quad_weights(points):
    index = np.arange(points)
    return np.pi / (points - 1) * np.sin(np.pi * index / (points - 1))


def parts_of(matrix):
    hi = matrix.astype(jnp.bfloat16)
    mid = (matrix - hi.astype(np.float32)).astype(jnp.bfloat16)
    return np.stack([hi, mid])


def constants(space, members):
    points = 4 * space
    diff = cheb_matrix(points).astype(np.float32)
    both = np.stack([np.eye(points, dtype=np.float32), diff]).reshape(2, space, 4, points)
    both = both.transpose(1, 0, 2, 3).reshape(2 * points, points)
    weight = quad_weights(points)
    root = np.sqrt(np.maximum(weight, 0.0))
    lane_w = np.zeros((members, 16, LANES), np.float32)
    lane_w[:, :9] = np.repeat(root, CH).reshape(members, 9, LANES)
    z_w = np.zeros((space, 8, LANES), np.float32)
    z_w[:, :4] = root.reshape(space, 4, 1)
    return parts_of(both), diff, parts_of(diff), lane_w, z_w


def mm(a, b, transpose_b=False):
    dims = (((1,), (1 if transpose_b else 0,)), ((), ()))
    return lax.dot_general(a, b, dims, precision=HIGHEST, preferred_element_type=jnp.float32)


def split(x):
    hi = x.astype(jnp.bfloat16)
    rest = x - hi.astype(jnp.float32)
    mid = rest.astype(jnp.bfloat16)
    lo = (rest - mid.astype(jnp.float32)).astype(jnp.bfloat16)
    return hi, mid, lo


def mm_bf(a, b, contract_b=0):
    dims = (((1,), (contract_b,)), ((), ()))
    return lax.dot_general(a, b, dims, preferred_element_type=jnp.float32)


def mm_exact(parts, b):
    return mm_bf(jnp.concatenate(parts, axis=1), b)


def iota(shape, axis):
    return lax.broadcasted_iota(jnp.int32, shape, axis)


def kernel(
    S,
    M,
    p_hbm,
    reg_hbm,
    v_hbm,
    a_hbm,
    dy_hbm,
    dp_hbm,
    wl_hbm,
    wz_hbm,
    f_loc,
    a_loc,
    outr_ref,
    outg_ref,
    p_ref,
    reg_ref,
    v_ref,
    a_ref,
    dy_ref,
    dp_ref,
    wl_ref,
    wz_ref,
    sel_p,
    sel_d,
    send_b,
    recv_b,
    tpose,
    own_x,
    gath_x,
    xz,
    ct,
    send_c,
    recv_c,
    coef,
    sbuf,
    dyq_b,
    tbuf,
    f_buf,
    g_buf,
    gp,
    gr,
    row,
    rows,
    send_sem,
    recv_sem,
    in_sem,
):
    N = 4 * S
    H = S // 2
    m = lax.axis_index("member")
    s = lax.axis_index("space")

    def wrap(value, size):
        return jnp.where(value >= size, value - size, value)

    def over_space(body):
        def step(k, carry):
            body(wrap(s + k, S))
            body(wrap(s + S - k, S))
            return carry

        lax.fori_loop(1, H, step, 0)
        body(wrap(s + H, S))

    def far_space(body):
        ny = S // 6
        core = lax.rem(s, 2)
        y = lax.rem(s // 2, ny)
        z = s // (2 * ny)

        def step(k, carry):
            column = wrap(z + lax.rem(k, 3), 3) * ny
            side = wrap(core + k // 3, 2)
            for dy in FAR[ny]:
                t = (column + wrap(y + dy, ny)) * 2 + side
                if dy == 0:

                    @pl.when(k != 0)
                    def _():
                        body(t)

                else:
                    body(t)
            return carry

        lax.fori_loop(0, 6, step, 0)

    def each_space(body):
        for k in range(1, H):
            body(wrap(s + k, S))
            body(wrap(s + S - k, S))
        body(wrap(s + H, S))

    def over_member(body):
        for k in range(1, M):
            body(wrap(m + k, M))

    def push(src, dst, which, member, space):
        pltpu.make_async_remote_copy(
            src_ref=src,
            dst_ref=dst,
            send_sem=send_sem.at[which],
            recv_sem=recv_sem.at[which],
            device_id=(member, space),
            device_id_type=MESH,
        ).start()

    def keep(src, dst, which):
        pltpu.make_async_copy(src, dst, recv_sem.at[which]).start()

    def arrived(ref, which):
        pltpu.make_async_copy(ref, ref, recv_sem.at[which]).wait()

    def sent(ref, which):
        pltpu.make_async_copy(ref, ref, send_sem.at[which]).wait()

    loads = [
        pltpu.make_async_copy(src, dst, in_sem.at[k])
        for k, (src, dst) in enumerate(
            (
                (v_hbm, v_ref),
                (p_hbm, p_ref),
                (a_hbm, a_ref),
                (dy_hbm, dy_ref),
                (dp_hbm, dp_ref),
                (reg_hbm, reg_ref),
                (wl_hbm.at[m], wl_ref),
                (wz_hbm.at[s], wz_ref),
            )
        )
    ]
    for load in loads:
        load.start()

    barrier = pltpu.get_barrier_semaphore()
    over_member(
        lambda t: pl.semaphore_signal(barrier, inc=1, device_id=(t, s), device_id_type=MESH)
    )
    each_space(
        lambda t: pl.semaphore_signal(barrier, inc=1, device_id=(m, t), device_id_type=MESH)
    )

    tpose[...] = jnp.zeros((LANES, LANES), jnp.float32)
    loads[0].wait()
    for c in range(3):
        tpose[4 * c : 4 * c + 4, 0:12] = v_ref[c]
    tpose[...] = tpose[...].T
    own_x[...] = (
        tpose[0:4, :]
        + pltpu.roll(tpose[4:8, :], 12, 1)
        + pltpu.roll(tpose[8:12, :], 24, 1)
    )
    loads[1].wait()
    loads[2].wait()
    q_hi, q_mid, q_lo = split(p_ref[...])
    send_b[...] = (
        (mm_bf(a_ref[0], q_lo, 1) + mm_bf(a_ref[1], q_hi, 1)) + mm_bf(a_ref[0], q_mid, 1)
    ) + mm_bf(a_ref[0], q_hi, 1)
    pl.semaphore_wait(barrier, S - 1 + M - 1)

    over_member(lambda t: push(own_x, gath_x.at[m], 0, t, s))
    keep(own_x, gath_x.at[m], 0)

    def bulk(first, last, which):
        mine = pl.ds(pl.multiple_of(8 * s, 8), 8)
        lanes = slice(first, last)

        def one(t):
            push(
                send_b.at[pl.ds(pl.multiple_of(8 * t, 8), 8), lanes],
                recv_b.at[mine, lanes],
                which,
                m,
                t,
            )

        far_space(one)
        keep(send_b.at[mine, lanes], recv_b.at[mine, lanes], which)

    bulk(0, 256, 1)

    group = iota((LANES, LANES), 0) // 4
    lane = iota((LANES, LANES), 1)
    comp = lane % 3
    kx = wave_step * (lane // 6 + 1).astype(jnp.float32)
    kx = jnp.where(lane % 6 < 3, kx, -kx)
    for z in range(4):
        chosen = [
            (group == 3 * z + 2).astype(jnp.float32),
            (group == 3 * z + 1).astype(jnp.float32),
            jnp.where(group == 3 * z, kx, 0.0),
            (group == 12 + 3 * z + comp).astype(jnp.float32),
        ]
        for k in range(4):
            one = chosen[k].astype(jnp.bfloat16)
            for i in range(3):
                sel_p[z, LANES * i : LANES * (i + 1), LANES * k : LANES * (k + 1)] = one
        one = (group == 3 * z + comp).astype(jnp.float32).astype(jnp.bfloat16)
        for i in range(3):
            sel_d[LANES * i : LANES * (i + 1), LANES * z : LANES * (z + 1)] = one
    for load in loads[3:]:
        load.wait()

    arrived(gath_x, 0)
    for k in range(M):
        piece = gath_x[k]
        for j in range(3):
            part = piece if j == 0 else pltpu.roll(piece, LANES - 12 * j, 1)
            xz[12 * k + 4 * j : 12 * k + 4 * j + 4, :] = part
    x = jnp.where(iota((N, LANES), 1) < 12, xz[...], 0.0)
    xz[...] = x
    x_hi, x_mid, x_lo = split(x)
    ct[...] = (
        (mm_bf(dp_ref[0], x_lo) + mm_bf(dp_ref[1], x_mid))
        + (mm_bf(dp_ref[0], x_mid) + mm_bf(dp_ref[1], x_hi))
    ) + mm_bf(dp_ref[0], x_hi)
    packed = xz[pl.ds(0, S, stride=4), :]
    for z in range(1, 4):
        packed = packed + pltpu.roll(xz[pl.ds(z, S, stride=4), :], 12 * z, 1)
    for z in range(4):
        packed = packed + pltpu.roll(ct[pl.ds(z, S, stride=4), :], 48 + 12 * z, 1)
    send_c[:, 0, :] = packed
    over_space(lambda t: push(send_c.at[t], recv_c.at[s], 2, m, t))
    keep(send_c.at[s], recv_c.at[s], 2)
    bulk(256, 384, 6)

    lane8 = iota((8, LANES), 1)

    def expand(last):
        def go(step, carry):
            for u in range(EXPAND):
                r = EXPAND * step + u
                base = pl.ds(pl.multiple_of(8 * r, 8), 8)
                v1 = recv_b[base, 128:256]
                if last:
                    v2 = recv_b[base, 256:384]
                    tiles = (
                        jnp.where(lane8 < 64, pltpu.roll(v1, 64, 1), pltpu.roll(v2, 64, 1)),
                        pltpu.roll(v2, 96, 1),
                    )
                else:
                    v0 = recv_b[base, 0:128]
                    tiles = (
                        v0,
                        jnp.where(lane8 < 32, pltpu.roll(v0, 32, 1), pltpu.roll(v1, 32, 1)),
                    )
                for i, v in enumerate(tiles):
                    at = 32 * r + 8 * (i + 2 * last)
                    sbuf[pl.ds(pl.multiple_of(at, 8), 8), :] = v
            return carry

        lax.fori_loop(0, S // EXPAND, go, 0)

    arrived(recv_b.at[:, 0:256], 1)
    expand(0)

    arrived(recv_c, 2)
    lane_s = iota((S, LANES), 1) % 4
    for k in range(4):
        xz[pl.ds(k, S, stride=4), :] = jnp.where(lane_s == k, recv_c[:, 0, :], 0.0)
    points = xz[...]
    dpoints = mm(dy_ref[...], points)
    parts = split(points)
    spread_y = mm_exact(split(dpoints), sel_d[...])
    for z in range(4):
        spread_p = mm_exact(parts, sel_p[z])
        for k in range(4):
            coef[k, z] = spread_p[:, LANES * k : LANES * (k + 1)]
        coef[4, z] = spread_y[:, LANES * z : LANES * (z + 1)]


    arrived(recv_b.at[:, 256:384], 6)
    expand(1)
    for pair in range(2):
        q2 = jnp.concatenate(
            [sbuf[pl.ds(2 * pair + i, N, stride=8), :] for i in range(2)], axis=1
        )
        q_hi, q_mid, _ = split(q2)
        dyq_b[pair] = (mm_bf(dp_ref[0], q_mid) + mm_bf(dp_ref[1], q_hi)) + mm_bf(dp_ref[0], q_hi)

    lane_n = iota((24, LANES), 1)
    lorentz = jnp.where(lane_n % 3 == 1, 0.0, lorentz_rate)
    real = lane_n % 6 < 3
    comp_n = lane_n % 3
    lane4 = iota((4, LANES), 1)
    z_rows = 4 * s + iota((4, 384), 0)
    z_mask = (z_rows > 0) & (z_rows < N - 1)
    lane_y = iota((4, 384), 1) // CH

    def slot_of(t):
        return pl.ds(pl.multiple_of(SLOT * t, 8), USED)

    def finish(step, carry):
        if M == 16:
            off = jnp.where(step < 4, step + 4, jnp.where(step < 6, step - 2, step - 6))
        else:
            off = step
        g = wrap(m // 2 + off, M // 2)
        at_y = pl.ds(pl.multiple_of(24 * g, 8), 24)
        for z in range(4):
            q = sbuf[pl.ds(192 * g + z, 24, stride=8), :]
            dzq = sbuf[pl.ds(192 * g + 4 + z, 24, stride=8), :]
            dyq = dyq_b[z // 2, at_y, LANES * (z % 2) : LANES * (z % 2 + 1)]
            up1 = pltpu.roll(q, LANES - 1, 1)
            up2 = pltpu.roll(q, LANES - 2, 1)
            down1 = pltpu.roll(q, 1, 1)
            qz = jnp.where(comp_n == 0, up2, jnp.where(comp_n == 1, up1, q))
            qy = jnp.where(comp_n == 0, up1, jnp.where(comp_n == 1, q, down1))
            other = jnp.where(real, pltpu.roll(q, LANES - 3, 1), pltpu.roll(q, 3, 1))
            tbuf[pl.ds(z, 24, stride=8), :] = (
                -coef[0, z, at_y, :] * dzq - qz * coef[3, z, at_y, :]
            ) + (
                -coef[1, z, at_y, :] * dyq
                + coef[2, z, at_y, :] * other
                - qy * coef[4, z, at_y, :]
                - lorentz * q
            )
        for h in range(2):
            slot = 2 * g + h
            base = pl.multiple_of(SLOT * slot, 8)
            for i in range(3):
                local = 3 * h + i
                r = 6 * g + local
                t = [tbuf[32 * local + 8 * k : 32 * local + 8 * k + 4, :] for k in range(4)]
                t1 = pltpu.roll(t[1], 96, 1)
                t2 = pltpu.roll(t[2], 64, 1)
                t3 = pltpu.roll(t[3], 32, 1)
                rhs = jnp.concatenate(
                    [
                        jnp.where(lane4 < 96, t[0], t1),
                        jnp.where(lane4 < 64, t1, t2),
                        jnp.where(lane4 < 32, t2, t3),
                    ],
                    axis=1,
                )
                at = pl.ds(pl.multiple_of(384 * r, 128), 384)
                y = 4 * r + lane_y
                mask = jnp.where(z_mask & (y > 0) & (y < N - 1), 1.0, 0.0)
                q = recv_b[pl.ds(pl.multiple_of(8 * r, 8), 4), :]
                acc = mask * (alpha_coef * reg_ref[:, at] + time_step * rhs)
                field = mask * (q + beta_coef * acc)
                a_loc[:, at] = acc
                f_loc[:, at] = field
                for l in range(3):
                    f_buf[pl.ds(base + 12 * i + 4 * l, 4), :] = field[:, 128 * l : 128 * l + 128]

            @pl.when(slot != m)
            def _():
                push(f_buf.at[slot_of(slot), :], g_buf.at[slot_of(m), :], 3, slot, s)

        return carry

    lax.fori_loop(0, M // 2, finish, 0)

    keep(f_buf.at[slot_of(m), :], g_buf.at[slot_of(m), :], 3)
    pick = (iota((16, N), 1) == 12 * m + iota((16, N), 0)).astype(jnp.float32)

    def fold(x):
        x = x + pltpu.roll(x, LANES - 1, 1)
        return x + pltpu.roll(x, LANES - 2, 1)

    here = fold(mm(pick, points))
    there = fold(mm(pick, dpoints))
    which = (iota((16, LANES), 1) // 4) % 3
    back4 = pltpu.roll(here, LANES - 4, 1)
    back8 = pltpu.roll(here, LANES - 8, 1)
    on4 = pltpu.roll(here, 4, 1)
    vel_w = jnp.where(which == 0, back8, jnp.where(which == 1, back4, here))
    vel_v = jnp.where(which == 0, back4, jnp.where(which == 1, here, on4))
    drag = jnp.where(which == 1, 0.0, lorentz_rate)
    dz_here = pltpu.roll(here, LANES - 48, 1)
    tpose[...] = jnp.zeros((LANES, LANES), jnp.float32)
    tpose[0:16, :] = -vel_w * dz_here + (-vel_v * there - drag * here)
    tpose[...] = tpose[...].T
    y_row = 12 * m + iota((1, 12), 1)
    for z in range(4):
        z_row = 4 * s + z
        inside = (y_row > 0) & (y_row < N - 1) & (z_row > 0) & (z_row < N - 1)
        for c in range(3):
            at = 12 * z + 4 * c
            value = tpose[at : at + 1, 0:12]
            outr_ref[c, z : z + 1, :] = time_step * jnp.where(inside, value, 0.0)

    gp[...] = jnp.zeros((M, 1, LANES), jnp.float32)
    arrived(g_buf.at[0 : USED * M, :], 3)
    values = []
    for t in range(9):
        weight_y = wl_ref[t : t + 1, :]
        for z in range(4):
            value = g_buf[pl.ds(4 * t + z, M, stride=SLOT), :]
            values.append(split(value * (weight_y * wz_ref[z : z + 1, :])))
    stack = jnp.concatenate(
        [jnp.concatenate([v[k] for v in values], axis=1) for k in range(3)], axis=0
    )
    nine = lax.dot_general(
        stack, stack, (((1,), (1,)), ((), ())), preferred_element_type=jnp.float32
    )
    three = (nine[2 * M : 3 * M] + nine[M : 2 * M]) + nine[0:M]
    part = (three[:, 2 * M : 3 * M] + three[:, M : 2 * M]) + three[:, 0:M]
    for k in range(M):
        gp[k, :, 0:M] = part[k : k + 1, :]
    over_member(lambda t: push(gp.at[t], gr.at[m], 4, t, s))
    keep(gp.at[m], gr.at[m], 4)
    arrived(gr, 4)
    row[...] = jnp.sum(gr[...], axis=0)
    each_space(lambda t: push(row, rows.at[s], 5, m, t))
    keep(row, rows.at[s], 5)
    arrived(rows, 5)
    outg_ref[...] = (jnp.sum(rows[...], axis=0) / CH)[:, 0:M]

    sent(gath_x.at[0 : M - 1], 0)
    sent(recv_b.at[0 : 8 * (S - 1), 0:256], 1)
    sent(recv_b.at[0 : 8 * (S - 1), 256:384], 6)
    sent(recv_c.at[0 : S - 1], 2)
    sent(g_buf.at[0 : USED * (M - 1), :], 3)
    sent(gr.at[0 : M - 1], 4)
    sent(rows.at[0 : S - 1], 5)


def copy_kernel(*refs):
    n = (len(refs) - 1) // 2
    stores = [pltpu.make_async_copy(refs[k], refs[n + k], refs[-1].at[k]) for k in range(n)]
    for store in stores:
        store.start()
    for store in stores:
        store.wait()


def handed_on(arrays):
    n = len(arrays)
    arrays = [pltpu.with_memory_space_constraint(a, pltpu.VMEM) for a in arrays]
    return pl.pallas_call(
        copy_kernel,
        out_shape=[jax.ShapeDtypeStruct(a.shape, a.dtype) for a in arrays],
        in_specs=[pl.BlockSpec(memory_space=pltpu.VMEM)] * n,
        out_specs=[pl.BlockSpec(memory_space=pl.ANY)] * n,
        scratch_shapes=[pltpu.SemaphoreType.DMA((n,))],
        name="hand_on",
    )(*arrays)


def shards(S, M, perturb, register, ref_velocity):
    N = 4 * S
    f32 = jnp.float32
    both, diff, diff_parts, lane_w, z_w = constants(S, M)
    vmem = pl.BlockSpec(memory_space=pltpu.VMEM)
    hbm = pl.BlockSpec(memory_space=pl.ANY)
    outs = pl.pallas_call(
        functools.partial(kernel, S, M),
        out_shape=(
            pltpu.VMEM((4, N * CH), f32),
            pltpu.VMEM((4, N * CH), f32),
            pltpu.VMEM((3, 4, 12), f32),
            pltpu.VMEM((1, M), f32),
        ),
        in_specs=[hbm] * 8,
        out_specs=(vmem,) * 4,
        scratch_shapes=[
            pltpu.VMEM((4 * CH, N), f32),
            pltpu.VMEM((4, N * CH), f32),
            pltpu.VMEM((3, 4, 12), f32),
            pltpu.VMEM((2, 2 * N, N), jnp.bfloat16),
            pltpu.VMEM((N, N), f32),
            pltpu.VMEM((2, N, N), jnp.bfloat16),
            pltpu.VMEM((16, LANES), f32),
            pltpu.VMEM((8, LANES), f32),
            pltpu.VMEM((4, 3 * LANES, 4 * LANES), jnp.bfloat16),
            pltpu.VMEM((3 * LANES, 4 * LANES), jnp.bfloat16),
            pltpu.VMEM((2 * N, 384), f32),
            pltpu.VMEM((2 * N, 384), f32),
            pltpu.VMEM((LANES, LANES), f32),
            pltpu.VMEM((4, LANES), f32),
            pltpu.VMEM((M, 4, LANES), f32),
            pltpu.VMEM((N, LANES), f32),
            pltpu.VMEM((N, LANES), f32),
            pltpu.VMEM((S, 1, LANES), f32),
            pltpu.VMEM((S, 1, LANES), f32),
            pltpu.VMEM((5, 4, N, LANES), f32),
            pltpu.VMEM((8 * N, LANES), f32),
            pltpu.VMEM((2, N, 2 * LANES), f32),
            pltpu.VMEM((8 * 24, LANES), f32),
            pltpu.VMEM((SLOT * M, LANES), f32),
            pltpu.VMEM((SLOT * M, LANES), f32),
            pltpu.VMEM((M, 1, LANES), f32),
            pltpu.VMEM((M, 1, LANES), f32),
            pltpu.VMEM((1, LANES), f32),
            pltpu.VMEM((S, 1, LANES), f32),
            pltpu.SemaphoreType.DMA((7,)),
            pltpu.SemaphoreType.DMA((7,)),
            pltpu.SemaphoreType.DMA((8,)),
        ],
        compiler_params=pltpu.CompilerParams(collective_id=0, has_side_effects=True),
        name="substep",
    )(
        perturb.reshape(4 * CH, N),
        register[0],
        ref_velocity,
        jnp.asarray(both),
        jnp.asarray(diff),
        jnp.asarray(diff_parts),
        jnp.asarray(lane_w),
        jnp.asarray(z_w),
    )
    fields, acc, ref_step, gram = handed_on(outs)
    return fields[None], acc[None], jnp.transpose(ref_step, (0, 2, 1)), gram


def solution(mesh):
    return jax.shard_map(
        functools.partial(shards, mesh.shape["space"], mesh.shape["member"]),
        mesh=mesh,
        in_specs=(
            P("member", "space", None, None),
            P("member", "space", None),
            P(None, "space", "member"),
        ),
        out_specs=(
            P("member", "space", None),
            P("member", "space", None),
            P(None, "member", "space"),
            P("member", None),
        ),
        check_vma=False,
    )
```

```python
import functools

import jax
import jax.numpy as jnp
import numpy as np
from jax import lax
from jax.experimental import pallas as pl
from jax.experimental.pallas import tpu as pltpu
from jax.sharding import PartitionSpec as P

MESH = pl.DeviceIdType.MESH
HIGHEST = lax.Precision.HIGHEST

time_step = 2e-05
alpha_coef = -5.0 / 9.0
beta_coef = 15.0 / 16.0
lorentz_rate = 25.0
wave_step = 0.5

CH = 96
LANES = 128
SLOT = 40
USED = 36
EXPAND = 6
FAR = {8: (4, 3, 5, 2, 6, 1, 7, 0), 1: (0,)}


def cheb_matrix(points):
    intervals = points - 1
    index = np.arange(points)
    nodes = np.cos(np.pi * index / intervals)
    signs = np.ones(points)
    signs[0] = 2.0
    signs[-1] = 2.0
    signs = signs * (-1.0) ** index
    spread = nodes[:, None] - nodes[None, :]
    matrix = signs[:, None] / signs[None, :] / (spread + np.eye(points))
    matrix = matrix - np.eye(points) * matrix.sum(axis=1)[:, None]
    return matrix


def quad_weights(points):
    index = np.arange(points)
    return np.pi / (points - 1) * np.sin(np.pi * index / (points - 1))


def parts_of(matrix):
    hi = matrix.astype(jnp.bfloat16)
    mid = (matrix - hi.astype(np.float32)).astype(jnp.bfloat16)
    return np.stack([hi, mid])


def constants(space, members):
    points = 4 * space
    diff = cheb_matrix(points).astype(np.float32)
    both = np.stack([np.eye(points, dtype=np.float32), diff]).reshape(2, space, 4, points)
    both = both.transpose(1, 0, 2, 3).reshape(2 * points, points)
    weight = quad_weights(points)
    root = np.sqrt(np.maximum(weight, 0.0))
    lane_w = np.zeros((members, 16, LANES), np.float32)
    lane_w[:, :9] = np.repeat(root, CH).reshape(members, 9, LANES)
    z_w = np.zeros((space, 8, LANES), np.float32)
    z_w[:, :4] = root.reshape(space, 4, 1)
    return parts_of(both), diff, parts_of(diff), lane_w, z_w


def mm(a, b, transpose_b=False):
    dims = (((1,), (1 if transpose_b else 0,)), ((), ()))
    return lax.dot_general(a, b, dims, precision=HIGHEST, preferred_element_type=jnp.float32)


def split(x):
    hi = x.astype(jnp.bfloat16)
    rest = x - hi.astype(jnp.float32)
    mid = rest.astype(jnp.bfloat16)
    lo = (rest - mid.astype(jnp.float32)).astype(jnp.bfloat16)
    return hi, mid, lo


def mm_bf(a, b, contract_b=0):
    dims = (((1,), (contract_b,)), ((), ()))
    return lax.dot_general(a, b, dims, preferred_element_type=jnp.float32)


def mm_exact(parts, b):
    return mm_bf(jnp.concatenate(parts, axis=1), b)


def iota(shape, axis):
    return lax.broadcasted_iota(jnp.int32, shape, axis)


def kernel(
    S,
    M,
    p_hbm,
    reg_hbm,
    v_hbm,
    a_hbm,
    dy_hbm,
    dp_hbm,
    wl_hbm,
    wz_hbm,
    f_loc,
    a_loc,
    outr_ref,
    outg_ref,
    p_ref,
    reg_ref,
    v_ref,
    a_ref,
    dy_ref,
    dp_ref,
    wl_ref,
    wz_ref,
    sel_p,
    sel_d,
    send_b,
    recv_b,
    tpose,
    own_x,
    gath_x,
    xz,
    ct,
    send_c,
    recv_c,
    coef,
    sbuf,
    dyq_b,
    tbuf,
    f_buf,
    g_buf,
    gp,
    gr,
    row,
    rows,
    send_sem,
    recv_sem,
    in_sem,
):
    N = 4 * S
    H = S // 2
    m = lax.axis_index("member")
    s = lax.axis_index("space")

    def wrap(value, size):
        return jnp.where(value >= size, value - size, value)

    def over_space(body):
        def step(k, carry):
            body(wrap(s + k, S))
            body(wrap(s + S - k, S))
            return carry

        lax.fori_loop(1, H, step, 0)
        body(wrap(s + H, S))

    def far_space(body):
        ny = S // 6
        core = lax.rem(s, 2)
        y = lax.rem(s // 2, ny)
        z = s // (2 * ny)

        def step(k, carry):
            column = wrap(z + lax.rem(k, 3), 3) * ny
            side = wrap(core + k // 3, 2)
            for dy in FAR[ny]:
                t = (column + wrap(y + dy, ny)) * 2 + side
                if dy == 0:

                    @pl.when(k != 0)
                    def _():
                        body(t)

                else:
                    body(t)
            return carry

        lax.fori_loop(0, 6, step, 0)

    def each_space(body):
        for k in range(1, H):
            body(wrap(s + k, S))
            body(wrap(s + S - k, S))
        body(wrap(s + H, S))

    def over_member(body):
        for k in range(1, M):
            body(wrap(m + k, M))

    def push(src, dst, which, member, space):
        pltpu.make_async_remote_copy(
            src_ref=src,
            dst_ref=dst,
            send_sem=send_sem.at[which],
            recv_sem=recv_sem.at[which],
            device_id=(member, space),
            device_id_type=MESH,
        ).start()

    def keep(src, dst, which):
        pltpu.make_async_copy(src, dst, recv_sem.at[which]).start()

    def arrived(ref, which):
        pltpu.make_async_copy(ref, ref, recv_sem.at[which]).wait()

    def sent(ref, which):
        pltpu.make_async_copy(ref, ref, send_sem.at[which]).wait()

    loads = [
        pltpu.make_async_copy(src, dst, in_sem.at[k])
        for k, (src, dst) in enumerate(
            (
                (v_hbm, v_ref),
                (p_hbm, p_ref),
                (a_hbm, a_ref),
                (dy_hbm, dy_ref),
                (dp_hbm, dp_ref),
                (reg_hbm, reg_ref),
                (wl_hbm.at[m], wl_ref),
                (wz_hbm.at[s], wz_ref),
            )
        )
    ]
    for load in loads:
        load.start()

    barrier = pltpu.get_barrier_semaphore()
    over_member(
        lambda t: pl.semaphore_signal(barrier, inc=1, device_id=(t, s), device_id_type=MESH)
    )
    each_space(
        lambda t: pl.semaphore_signal(barrier, inc=1, device_id=(m, t), device_id_type=MESH)
    )

    tpose[...] = jnp.zeros((LANES, LANES), jnp.float32)
    loads[0].wait()
    for c in range(3):
        tpose[4 * c : 4 * c + 4, 0:12] = v_ref[c]
    tpose[...] = tpose[...].T
    own_x[...] = (
        tpose[0:4, :]
        + pltpu.roll(tpose[4:8, :], 12, 1)
        + pltpu.roll(tpose[8:12, :], 24, 1)
    )
    loads[1].wait()
    loads[2].wait()
    q_hi, q_mid, q_lo = split(p_ref[...])
    send_b[...] = (
        (mm_bf(a_ref[0], q_lo, 1) + mm_bf(a_ref[1], q_hi, 1)) + mm_bf(a_ref[0], q_mid, 1)
    ) + mm_bf(a_ref[0], q_hi, 1)
    pl.semaphore_wait(barrier, S - 1 + M - 1)

    over_member(lambda t: push(own_x, gath_x.at[m], 0, t, s))
    keep(own_x, gath_x.at[m], 0)

    def bulk(first, last, which):
        mine = pl.ds(pl.multiple_of(8 * s, 8), 8)
        lanes = slice(first, last)

        def one(t):
            push(
                send_b.at[pl.ds(pl.multiple_of(8 * t, 8), 8), lanes],
                recv_b.at[mine, lanes],
                which,
                m,
                t,
            )

        far_space(one)
        keep(send_b.at[mine, lanes], recv_b.at[mine, lanes], which)

    bulk(0, 256, 1)

    group = iota((LANES, LANES), 0) // 4
    lane = iota((LANES, LANES), 1)
    comp = lane % 3
    kx = wave_step * (lane // 6 + 1).astype(jnp.float32)
    kx = jnp.where(lane % 6 < 3, kx, -kx)
    for z in range(4):
        chosen = [
            (group == 3 * z + 2).astype(jnp.float32),
            (group == 3 * z + 1).astype(jnp.float32),
            jnp.where(group == 3 * z, kx, 0.0),
            (group == 12 + 3 * z + comp).astype(jnp.float32),
        ]
        for k in range(4):
            one = chosen[k].astype(jnp.bfloat16)
            for i in range(3):
                sel_p[z, LANES * i : LANES * (i + 1), LANES * k : LANES * (k + 1)] = one
        one = (group == 3 * z + comp).astype(jnp.float32).astype(jnp.bfloat16)
        for i in range(3):
            sel_d[LANES * i : LANES * (i + 1), LANES * z : LANES * (z + 1)] = one
    for load in loads[3:]:
        load.wait()

    arrived(gath_x, 0)
    for k in range(M):
        piece = gath_x[k]
        for j in range(3):
            part = piece if j == 0 else pltpu.roll(piece, LANES - 12 * j, 1)
            xz[12 * k + 4 * j : 12 * k + 4 * j + 4, :] = part
    x = jnp.where(iota((N, LANES), 1) < 12, xz[...], 0.0)
    xz[...] = x
    x_hi, x_mid, x_lo = split(x)
    ct[...] = (
        (mm_bf(dp_ref[0], x_lo) + mm_bf(dp_ref[1], x_mid))
        + (mm_bf(dp_ref[0], x_mid) + mm_bf(dp_ref[1], x_hi))
    ) + mm_bf(dp_ref[0], x_hi)
    packed = xz[pl.ds(0, S, stride=4), :]
    for z in range(1, 4):
        packed = packed + pltpu.roll(xz[pl.ds(z, S, stride=4), :], 12 * z, 1)
    for z in range(4):
        packed = packed + pltpu.roll(ct[pl.ds(z, S, stride=4), :], 48 + 12 * z, 1)
    send_c[:, 0, :] = packed
    over_space(lambda t: push(send_c.at[t], recv_c.at[s], 2, m, t))
    keep(send_c.at[s], recv_c.at[s], 2)
    bulk(256, 384, 6)

    lane8 = iota((8, LANES), 1)

    def expand(last):
        def go(step, carry):
            for u in range(EXPAND):
                r = EXPAND * step + u
                base = pl.ds(pl.multiple_of(8 * r, 8), 8)
                v1 = recv_b[base, 128:256]
                if last:
                    v2 = recv_b[base, 256:384]
                    tiles = (
                        jnp.where(lane8 < 64, pltpu.roll(v1, 64, 1), pltpu.roll(v2, 64, 1)),
                        pltpu.roll(v2, 96, 1),
                    )
                else:
                    v0 = recv_b[base, 0:128]
                    tiles = (
                        v0,
                        jnp.where(lane8 < 32, pltpu.roll(v0, 32, 1), pltpu.roll(v1, 32, 1)),
                    )
                for i, v in enumerate(tiles):
                    at = 32 * r + 8 * (i + 2 * last)
                    sbuf[pl.ds(pl.multiple_of(at, 8), 8), :] = v
            return carry

        lax.fori_loop(0, S // EXPAND, go, 0)

    arrived(recv_b.at[:, 0:256], 1)
    expand(0)

    arrived(recv_c, 2)
    lane_s = iota((S, LANES), 1) % 4
    for k in range(4):
        xz[pl.ds(k, S, stride=4), :] = jnp.where(lane_s == k, recv_c[:, 0, :], 0.0)
    points = xz[...]
    dpoints = mm(dy_ref[...], points)
    parts = split(points)
    spread_y = mm_exact(split(dpoints), sel_d[...])
    for z in range(4):
        spread_p = mm_exact(parts, sel_p[z])
        for k in range(4):
            coef[k, z] = spread_p[:, LANES * k : LANES * (k + 1)]
        coef[4, z] = spread_y[:, LANES * z : LANES * (z + 1)]


    arrived(recv_b.at[:, 256:384], 6)
    expand(1)
    for pair in range(2):
        q2 = jnp.concatenate(
            [sbuf[pl.ds(2 * pair + i, N, stride=8), :] for i in range(2)], axis=1
        )
        q_hi, q_mid, _ = split(q2)
        dyq_b[pair] = (mm_bf(dp_ref[0], q_mid) + mm_bf(dp_ref[1], q_hi)) + mm_bf(dp_ref[0], q_hi)

    lane_n = iota((24, LANES), 1)
    lorentz = jnp.where(lane_n % 3 == 1, 0.0, lorentz_rate)
    real = lane_n % 6 < 3
    comp_n = lane_n % 3
    lane4 = iota((4, LANES), 1)
    z_rows = 4 * s + iota((4, 384), 0)
    z_mask = (z_rows > 0) & (z_rows < N - 1)
    lane_y = iota((4, 384), 1) // CH

    def slot_of(t):
        return pl.ds(pl.multiple_of(SLOT * t, 8), USED)

    def finish(step, carry):
        if M == 16:
            off = jnp.where(step < 4, step + 4, jnp.where(step < 6, step - 2, step - 6))
        else:
            off = step
        g = wrap(m // 2 + off, M // 2)
        at_y = pl.ds(pl.multiple_of(24 * g, 8), 24)
        for z in range(4):
            q = sbuf[pl.ds(192 * g + z, 24, stride=8), :]
            dzq = sbuf[pl.ds(192 * g + 4 + z, 24, stride=8), :]
            dyq = dyq_b[z // 2, at_y, LANES * (z % 2) : LANES * (z % 2 + 1)]
            up1 = pltpu.roll(q, LANES - 1, 1)
            up2 = pltpu.roll(q, LANES - 2, 1)
            down1 = pltpu.roll(q, 1, 1)
            qz = jnp.where(comp_n == 0, up2, jnp.where(comp_n == 1, up1, q))
            qy = jnp.where(comp_n == 0, up1, jnp.where(comp_n == 1, q, down1))
            other = jnp.where(real, pltpu.roll(q, LANES - 3, 1), pltpu.roll(q, 3, 1))
            tbuf[pl.ds(z, 24, stride=8), :] = (
                -coef[0, z, at_y, :] * dzq - qz * coef[3, z, at_y, :]
            ) + (
                -coef[1, z, at_y, :] * dyq
                + coef[2, z, at_y, :] * other
                - qy * coef[4, z, at_y, :]
                - lorentz * q
            )
        for h in range(2):
            slot = 2 * g + h
            base = pl.multiple_of(SLOT * slot, 8)
            for i in range(3):
                local = 3 * h + i
                r = 6 * g + local
                t = [tbuf[32 * local + 8 * k : 32 * local + 8 * k + 4, :] for k in range(4)]
                t1 = pltpu.roll(t[1], 96, 1)
                t2 = pltpu.roll(t[2], 64, 1)
                t3 = pltpu.roll(t[3], 32, 1)
                rhs = jnp.concatenate(
                    [
                        jnp.where(lane4 < 96, t[0], t1),
                        jnp.where(lane4 < 64, t1, t2),
                        jnp.where(lane4 < 32, t2, t3),
                    ],
                    axis=1,
                )
                at = pl.ds(pl.multiple_of(384 * r, 128), 384)
                y = 4 * r + lane_y
                mask = jnp.where(z_mask & (y > 0) & (y < N - 1), 1.0, 0.0)
                q = recv_b[pl.ds(pl.multiple_of(8 * r, 8), 4), :]
                acc = mask * (alpha_coef * reg_ref[:, at] + time_step * rhs)
                field = mask * (q + beta_coef * acc)
                a_loc[:, at] = acc
                f_loc[:, at] = field
                for l in range(3):
                    f_buf[pl.ds(base + 12 * i + 4 * l, 4), :] = field[:, 128 * l : 128 * l + 128]

            @pl.when(slot != m)
            def _():
                push(f_buf.at[slot_of(slot), :], g_buf.at[slot_of(m), :], 3, slot, s)

        return carry

    lax.fori_loop(0, M // 2, finish, 0)

    keep(f_buf.at[slot_of(m), :], g_buf.at[slot_of(m), :], 3)
    pick = (iota((16, N), 1) == 12 * m + iota((16, N), 0)).astype(jnp.float32)

    def fold(x):
        x = x + pltpu.roll(x, LANES - 1, 1)
        return x + pltpu.roll(x, LANES - 2, 1)

    here = fold(mm(pick, points))
    there = fold(mm(pick, dpoints))
    which = (iota((16, LANES), 1) // 4) % 3
    back4 = pltpu.roll(here, LANES - 4, 1)
    back8 = pltpu.roll(here, LANES - 8, 1)
    on4 = pltpu.roll(here, 4, 1)
    vel_w = jnp.where(which == 0, back8, jnp.where(which == 1, back4, here))
    vel_v = jnp.where(which == 0, back4, jnp.where(which == 1, here, on4))
    drag = jnp.where(which == 1, 0.0, lorentz_rate)
    dz_here = pltpu.roll(here, LANES - 48, 1)
    tpose[...] = jnp.zeros((LANES, LANES), jnp.float32)
    tpose[0:16, :] = -vel_w * dz_here + (-vel_v * there - drag * here)
    tpose[...] = tpose[...].T
    y_row = 12 * m + iota((1, 12), 1)
    for z in range(4):
        z_row = 4 * s + z
        inside = (y_row > 0) & (y_row < N - 1) & (z_row > 0) & (z_row < N - 1)
        for c in range(3):
            at = 12 * z + 4 * c
            value = tpose[at : at + 1, 0:12]
            outr_ref[c, z : z + 1, :] = time_step * jnp.where(inside, value, 0.0)

    gp[...] = jnp.zeros((2, LANES), jnp.float32)
    arrived(g_buf.at[0 : USED * M, :], 3)
    values = []
    for t in range(9):
        weight_y = wl_ref[t : t + 1, :]
        for z in range(4):
            value = g_buf[pl.ds(4 * t + z, M, stride=SLOT), :]
            values.append(split(value * (weight_y * wz_ref[z : z + 1, :])))
    stack = jnp.concatenate(
        [jnp.concatenate([v[k] for v in values], axis=1) for k in range(3)], axis=0
    )
    nine = lax.dot_general(
        stack, stack, (((1,), (1,)), ((), ())), preferred_element_type=jnp.float32
    )
    three = (nine[2 * M : 3 * M] + nine[M : 2 * M]) + nine[0:M]
    part = (three[:, 2 * M : 3 * M] + three[:, M : 2 * M]) + three[:, 0:M]
    for k in range(M):
        at, lane = divmod(M * k, LANES)
        gp[at : at + 1, lane : lane + M] = part[k : k + 1, :]
    nx, ny = min(4, M), S // 6
    z_hi, x_at = m // nx, lax.rem(m, nx)
    z_lo, y_at, core = s // (2 * ny), lax.rem(s // 2, ny), lax.rem(s, 2)
    mine = (x_at * ny + y_at) * 2 + core
    column, sides = z_lo * ny, (core, 1 - core)
    for dy in FAR[ny]:
        y_to = column + wrap(y_at + dy, ny)
        for dx in sorted(range(nx), key=lambda d: -min(d, nx - d)):
            to = z_hi * nx + wrap(x_at + dx, nx)
            for side in (1, 0):
                if dy or dx or side:
                    push(gp, gr.at[mine], 4, to, y_to * 2 + sides[side])
    keep(gp, gr.at[mine], 4)
    arrived(gr, 4)
    row[...] = jnp.sum(gr[...], axis=0)
    n_hi = M // nx
    level = z_hi * 3 + z_lo
    for dh in sorted(range(n_hi), key=lambda d: -min(d, n_hi - d)):
        to = wrap(z_hi + dh, n_hi) * nx + x_at
        for dl in (1, 2, 0):
            if dh or dl:
                push(row, rows.at[level], 5, to, (wrap(z_lo + dl, 3) * ny + y_at) * 2 + core)
    keep(row, rows.at[level], 5)
    arrived(rows, 5)
    total = jnp.sum(rows[...], axis=0) / CH
    found = jnp.zeros((1, M), jnp.float32)
    for k in range(M):
        at, lane = divmod(M * k, LANES)
        found = jnp.where(m == k, total[at : at + 1, lane : lane + M], found)
    outg_ref[...] = found

    sent(gath_x.at[0 : M - 1], 0)
    sent(recv_b.at[0 : 8 * (S - 1), 0:256], 1)
    sent(recv_b.at[0 : 8 * (S - 1), 256:384], 6)
    sent(recv_c.at[0 : S - 1], 2)
    sent(g_buf.at[0 : USED * (M - 1), :], 3)
    sent(gr.at[0 : 2 * nx * ny - 1], 4)
    sent(rows.at[0 : 3 * n_hi - 1], 5)


def copy_kernel(*refs):
    n = (len(refs) - 1) // 2
    stores = [pltpu.make_async_copy(refs[k], refs[n + k], refs[-1].at[k]) for k in range(n)]
    for store in stores:
        store.start()
    for store in stores:
        store.wait()


def handed_on(arrays):
    n = len(arrays)
    arrays = [pltpu.with_memory_space_constraint(a, pltpu.VMEM) for a in arrays]
    return pl.pallas_call(
        copy_kernel,
        out_shape=[jax.ShapeDtypeStruct(a.shape, a.dtype) for a in arrays],
        in_specs=[pl.BlockSpec(memory_space=pltpu.VMEM)] * n,
        out_specs=[pl.BlockSpec(memory_space=pl.ANY)] * n,
        scratch_shapes=[pltpu.SemaphoreType.DMA((n,))],
        name="hand_on",
    )(*arrays)


def shards(S, M, perturb, register, ref_velocity):
    N = 4 * S
    f32 = jnp.float32
    both, diff, diff_parts, lane_w, z_w = constants(S, M)
    vmem = pl.BlockSpec(memory_space=pltpu.VMEM)
    hbm = pl.BlockSpec(memory_space=pl.ANY)
    outs = pl.pallas_call(
        functools.partial(kernel, S, M),
        out_shape=(
            pltpu.VMEM((4, N * CH), f32),
            pltpu.VMEM((4, N * CH), f32),
            pltpu.VMEM((3, 4, 12), f32),
            pltpu.VMEM((1, M), f32),
        ),
        in_specs=[hbm] * 8,
        out_specs=(vmem,) * 4,
        scratch_shapes=[
            pltpu.VMEM((4 * CH, N), f32),
            pltpu.VMEM((4, N * CH), f32),
            pltpu.VMEM((3, 4, 12), f32),
            pltpu.VMEM((2, 2 * N, N), jnp.bfloat16),
            pltpu.VMEM((N, N), f32),
            pltpu.VMEM((2, N, N), jnp.bfloat16),
            pltpu.VMEM((16, LANES), f32),
            pltpu.VMEM((8, LANES), f32),
            pltpu.VMEM((4, 3 * LANES, 4 * LANES), jnp.bfloat16),
            pltpu.VMEM((3 * LANES, 4 * LANES), jnp.bfloat16),
            pltpu.VMEM((2 * N, 384), f32),
            pltpu.VMEM((2 * N, 384), f32),
            pltpu.VMEM((LANES, LANES), f32),
            pltpu.VMEM((4, LANES), f32),
            pltpu.VMEM((M, 4, LANES), f32),
            pltpu.VMEM((N, LANES), f32),
            pltpu.VMEM((N, LANES), f32),
            pltpu.VMEM((S, 1, LANES), f32),
            pltpu.VMEM((S, 1, LANES), f32),
            pltpu.VMEM((5, 4, N, LANES), f32),
            pltpu.VMEM((8 * N, LANES), f32),
            pltpu.VMEM((2, N, 2 * LANES), f32),
            pltpu.VMEM((8 * 24, LANES), f32),
            pltpu.VMEM((SLOT * M, LANES), f32),
            pltpu.VMEM((SLOT * M, LANES), f32),
            pltpu.VMEM((2, LANES), f32),
            pltpu.VMEM((min(4, M) * S // 3, 2, LANES), f32),
            pltpu.VMEM((2, LANES), f32),
            pltpu.VMEM((3 * (M // min(4, M)), 2, LANES), f32),
            pltpu.SemaphoreType.DMA((7,)),
            pltpu.SemaphoreType.DMA((7,)),
            pltpu.SemaphoreType.DMA((8,)),
        ],
        compiler_params=pltpu.CompilerParams(collective_id=0, has_side_effects=True),
        name="substep",
    )(
        perturb.reshape(4 * CH, N),
        register[0],
        ref_velocity,
        jnp.asarray(both),
        jnp.asarray(diff),
        jnp.asarray(diff_parts),
        jnp.asarray(lane_w),
        jnp.asarray(z_w),
    )
    fields, acc, ref_step, gram = handed_on(outs)
    return fields[None], acc[None], jnp.transpose(ref_step, (0, 2, 1)), gram


def solution(mesh):
    return jax.shard_map(
        functools.partial(shards, mesh.shape["space"], mesh.shape["member"]),
        mesh=mesh,
        in_specs=(
            P("member", "space", None, None),
            P("member", "space", None),
            P(None, "space", "member"),
        ),
        out_specs=(
            P("member", "space", None),
            P("member", "space", None),
            P(None, "member", "space"),
            P("member", None),
        ),
        check_vma=False,
    )
```

```python
import functools

import jax
import jax.numpy as jnp
import numpy as np
from jax import lax
from jax.experimental import pallas as pl
from jax.experimental.pallas import tpu as pltpu
from jax.sharding import PartitionSpec as P

MESH = pl.DeviceIdType.MESH
HIGHEST = lax.Precision.HIGHEST

time_step = 2e-05
alpha_coef = -5.0 / 9.0
beta_coef = 15.0 / 16.0
lorentz_rate = 25.0
wave_step = 0.5

CH = 96
LANES = 128
SLOT = 40
USED = 36
EXPAND = 6
FAR = {8: (4, 3, 5, 2, 6, 1, 7, 0), 1: (0,)}


def cheb_matrix(points):
    intervals = points - 1
    index = np.arange(points)
    nodes = np.cos(np.pi * index / intervals)
    signs = np.ones(points)
    signs[0] = 2.0
    signs[-1] = 2.0
    signs = signs * (-1.0) ** index
    spread = nodes[:, None] - nodes[None, :]
    matrix = signs[:, None] / signs[None, :] / (spread + np.eye(points))
    matrix = matrix - np.eye(points) * matrix.sum(axis=1)[:, None]
    return matrix


def quad_weights(points):
    index = np.arange(points)
    return np.pi / (points - 1) * np.sin(np.pi * index / (points - 1))


def parts_of(matrix):
    hi = matrix.astype(jnp.bfloat16)
    mid = (matrix - hi.astype(np.float32)).astype(jnp.bfloat16)
    return np.stack([hi, mid])


def constants(space, members):
    points = 4 * space
    diff = cheb_matrix(points).astype(np.float32)
    both = np.stack([np.eye(points, dtype=np.float32), diff]).reshape(2, space, 4, points)
    both = both.transpose(1, 0, 2, 3).reshape(2 * points, points)
    weight = quad_weights(points)
    root = np.sqrt(np.maximum(weight, 0.0))
    lane_w = np.zeros((members, 16, LANES), np.float32)
    lane_w[:, :9] = np.repeat(root, CH).reshape(members, 9, LANES)
    z_w = np.zeros((space, 8, LANES), np.float32)
    z_w[:, :4] = root.reshape(space, 4, 1)
    return parts_of(both), parts_of(diff), lane_w, z_w


def mm(a, b, transpose_b=False):
    dims = (((1,), (1 if transpose_b else 0,)), ((), ()))
    return lax.dot_general(a, b, dims, precision=HIGHEST, preferred_element_type=jnp.float32)


def split(x):
    hi = x.astype(jnp.bfloat16)
    rest = x - hi.astype(jnp.float32)
    mid = rest.astype(jnp.bfloat16)
    lo = (rest - mid.astype(jnp.float32)).astype(jnp.bfloat16)
    return hi, mid, lo


def mm_bf(a, b, contract_b=0):
    dims = (((1,), (contract_b,)), ((), ()))
    return lax.dot_general(a, b, dims, preferred_element_type=jnp.float32)


def mm_exact(parts, b):
    return mm_bf(jnp.concatenate(parts, axis=1), b)


def iota(shape, axis):
    return lax.broadcasted_iota(jnp.int32, shape, axis)


def kernel(
    S,
    M,
    p_hbm,
    reg_hbm,
    v_hbm,
    a_hbm,
    dp_hbm,
    wl_hbm,
    wz_hbm,
    f_loc,
    a_loc,
    outr_ref,
    outg_ref,
    p_ref,
    reg_ref,
    v_ref,
    a_ref,
    dp_ref,
    wl_ref,
    wz_ref,
    sel_p,
    sel_d,
    send_b,
    recv_b,
    tpose,
    own_x,
    gath_x,
    xz,
    ct,
    send_c,
    recv_c,
    coef,
    sbuf,
    dyq_b,
    tbuf,
    f_buf,
    g_buf,
    gp,
    gr,
    row,
    rows,
    send_sem,
    recv_sem,
    in_sem,
):
    N = 4 * S
    H = S // 2
    m = lax.axis_index("member")
    s = lax.axis_index("space")

    def wrap(value, size):
        return jnp.where(value >= size, value - size, value)

    def over_space(body):
        def step(k, carry):
            body(wrap(s + k, S))
            body(wrap(s + S - k, S))
            return carry

        lax.fori_loop(1, H, step, 0)
        body(wrap(s + H, S))

    def far_space(body):
        ny = S // 6
        core = lax.rem(s, 2)
        y = lax.rem(s // 2, ny)
        z = s // (2 * ny)

        def step(k, carry):
            column = wrap(z + lax.rem(k, 3), 3) * ny
            side = wrap(core + k // 3, 2)
            for dy in FAR[ny]:
                t = (column + wrap(y + dy, ny)) * 2 + side
                if dy == 0:

                    @pl.when(k != 0)
                    def _():
                        body(t)

                else:
                    body(t)
            return carry

        lax.fori_loop(0, 6, step, 0)

    def each_space(body):
        ny = S // 6
        core = lax.rem(s, 2)
        y = lax.rem(s // 2, ny)
        z = s // (2 * ny)
        columns = [wrap(z + dz, 3) * ny for dz in range(3)]
        sides = [core, 1 - core]
        for dy in FAR[ny]:
            at = wrap(y + dy, ny)
            for dz in (1, 2, 0):
                for side in (1, 0):
                    if dy or dz or side:
                        body((columns[dz] + at) * 2 + sides[side])

    def over_member(body):
        for k in range(1, M):
            body(wrap(m + k, M))

    def push(src, dst, which, member, space):
        pltpu.make_async_remote_copy(
            src_ref=src,
            dst_ref=dst,
            send_sem=send_sem.at[which],
            recv_sem=recv_sem.at[which],
            device_id=(member, space),
            device_id_type=MESH,
        ).start()

    def keep(src, dst, which):
        pltpu.make_async_copy(src, dst, recv_sem.at[which]).start()

    def arrived(ref, which):
        pltpu.make_async_copy(ref, ref, recv_sem.at[which]).wait()

    def sent(ref, which):
        pltpu.make_async_copy(ref, ref, send_sem.at[which]).wait()

    loads = [
        pltpu.make_async_copy(src, dst, in_sem.at[k])
        for k, (src, dst) in enumerate(
            (
                (v_hbm, v_ref),
                (p_hbm, p_ref),
                (a_hbm, a_ref),
                (dp_hbm, dp_ref),
                (reg_hbm, reg_ref),
                (wl_hbm.at[m], wl_ref),
                (wz_hbm.at[s], wz_ref),
            )
        )
    ]
    for load in loads:
        load.start()

    barrier = pltpu.get_barrier_semaphore()
    each_space(
        lambda t: pl.semaphore_signal(barrier, inc=1, device_id=(m, t), device_id_type=MESH)
    )
    over_member(
        lambda t: pl.semaphore_signal(barrier, inc=1, device_id=(t, s), device_id_type=MESH)
    )

    tpose[...] = jnp.zeros((LANES, LANES), jnp.float32)
    loads[0].wait()
    for c in range(3):
        tpose[4 * c : 4 * c + 4, 0:12] = v_ref[c]
    tpose[...] = tpose[...].T
    own_x[...] = (
        tpose[0:4, :]
        + pltpu.roll(tpose[4:8, :], 12, 1)
        + pltpu.roll(tpose[8:12, :], 24, 1)
    )
    loads[1].wait()
    loads[2].wait()
    q_hi, q_mid, q_lo = split(p_ref[...])
    send_b[...] = (
        (mm_bf(a_ref[0], q_lo, 1) + mm_bf(a_ref[1], q_hi, 1)) + mm_bf(a_ref[0], q_mid, 1)
    ) + mm_bf(a_ref[0], q_hi, 1)
    pl.semaphore_wait(barrier, S - 1 + M - 1)

    over_member(lambda t: push(own_x, gath_x.at[m], 0, t, s))
    keep(own_x, gath_x.at[m], 0)

    def bulk(first, last, which):
        mine = pl.ds(pl.multiple_of(8 * s, 8), 8)
        lanes = slice(first, last)

        def one(t):
            push(
                send_b.at[pl.ds(pl.multiple_of(8 * t, 8), 8), lanes],
                recv_b.at[mine, lanes],
                which,
                m,
                t,
            )

        far_space(one)
        keep(send_b.at[mine, lanes], recv_b.at[mine, lanes], which)

    bulk(0, 256, 1)

    group = iota((LANES, LANES), 0) // 4
    lane = iota((LANES, LANES), 1)
    comp = lane % 3
    kx = wave_step * (lane // 6 + 1).astype(jnp.float32)
    kx = jnp.where(lane % 6 < 3, kx, -kx)
    for z in range(4):
        chosen = [
            (group == 3 * z + 2).astype(jnp.float32),
            (group == 3 * z + 1).astype(jnp.float32),
            jnp.where(group == 3 * z, kx, 0.0),
            (group == 12 + 3 * z + comp).astype(jnp.float32),
        ]
        for k in range(4):
            one = chosen[k].astype(jnp.bfloat16)
            for i in range(3):
                sel_p[z, LANES * i : LANES * (i + 1), LANES * k : LANES * (k + 1)] = one
        one = (group == 3 * z + comp).astype(jnp.float32).astype(jnp.bfloat16)
        for i in range(3):
            sel_d[LANES * i : LANES * (i + 1), LANES * z : LANES * (z + 1)] = one
    for load in loads[3:]:
        load.wait()

    arrived(gath_x, 0)
    for k in range(M):
        piece = gath_x[k]
        for j in range(3):
            part = piece if j == 0 else pltpu.roll(piece, LANES - 12 * j, 1)
            xz[12 * k + 4 * j : 12 * k + 4 * j + 4, :] = part
    x = jnp.where(iota((N, LANES), 1) < 12, xz[...], 0.0)
    xz[...] = x
    def slope(parts):
        hi, mid, lo = parts
        return (
            (mm_bf(dp_ref[0], lo) + mm_bf(dp_ref[1], mid))
            + (mm_bf(dp_ref[0], mid) + mm_bf(dp_ref[1], hi))
        ) + mm_bf(dp_ref[0], hi)

    ct[...] = slope(split(x))
    packed = xz[pl.ds(0, S, stride=4), :]
    for z in range(1, 4):
        packed = packed + pltpu.roll(xz[pl.ds(z, S, stride=4), :], 12 * z, 1)
    for z in range(4):
        packed = packed + pltpu.roll(ct[pl.ds(z, S, stride=4), :], 48 + 12 * z, 1)
    send_c[:, 0, :] = packed
    over_space(lambda t: push(send_c.at[t], recv_c.at[s], 2, m, t))
    keep(send_c.at[s], recv_c.at[s], 2)
    bulk(256, 384, 6)

    lane8 = iota((8, LANES), 1)

    def expand(last):
        def go(step, carry):
            for u in range(EXPAND):
                r = EXPAND * step + u
                base = pl.ds(pl.multiple_of(8 * r, 8), 8)
                v1 = recv_b[base, 128:256]
                if last:
                    v2 = recv_b[base, 256:384]
                    tiles = (
                        jnp.where(lane8 < 64, pltpu.roll(v1, 64, 1), pltpu.roll(v2, 64, 1)),
                        pltpu.roll(v2, 96, 1),
                    )
                else:
                    v0 = recv_b[base, 0:128]
                    tiles = (
                        v0,
                        jnp.where(lane8 < 32, pltpu.roll(v0, 32, 1), pltpu.roll(v1, 32, 1)),
                    )
                for i, v in enumerate(tiles):
                    at = 32 * r + 8 * (i + 2 * last)
                    sbuf[pl.ds(pl.multiple_of(at, 8), 8), :] = v
            return carry

        lax.fori_loop(0, S // EXPAND, go, 0)

    arrived(recv_b.at[:, 0:256], 1)
    expand(0)

    arrived(recv_c, 2)
    lane_s = iota((S, LANES), 1) % 4
    for k in range(4):
        xz[pl.ds(k, S, stride=4), :] = jnp.where(lane_s == k, recv_c[:, 0, :], 0.0)
    points = xz[...]
    parts = split(points)
    dpoints = slope(parts)
    spread_y = mm_exact(split(dpoints), sel_d[...])
    for z in range(4):
        spread_p = mm_exact(parts, sel_p[z])
        for k in range(4):
            coef[k, z] = spread_p[:, LANES * k : LANES * (k + 1)]
        coef[4, z] = spread_y[:, LANES * z : LANES * (z + 1)]


    arrived(recv_b.at[:, 256:384], 6)
    expand(1)
    for pair in range(2):
        q2 = jnp.concatenate(
            [sbuf[pl.ds(2 * pair + i, N, stride=8), :] for i in range(2)], axis=1
        )
        q_hi, q_mid, _ = split(q2)
        dyq_b[pair] = (mm_bf(dp_ref[0], q_mid) + mm_bf(dp_ref[1], q_hi)) + mm_bf(dp_ref[0], q_hi)

    lane_n = iota((24, LANES), 1)
    lorentz = jnp.where(lane_n % 3 == 1, 0.0, lorentz_rate)
    real = lane_n % 6 < 3
    comp_n = lane_n % 3
    lane4 = iota((4, LANES), 1)
    z_rows = 4 * s + iota((4, 384), 0)
    z_mask = (z_rows > 0) & (z_rows < N - 1)
    lane_y = iota((4, 384), 1) // CH

    def slot_of(t):
        return pl.ds(pl.multiple_of(SLOT * t, 8), USED)

    def finish(step, carry):
        if M == 16:
            off = jnp.where(step < 4, step + 4, jnp.where(step < 6, step - 2, step - 6))
        else:
            off = step
        g = wrap(m // 2 + off, M // 2)
        at_y = pl.ds(pl.multiple_of(24 * g, 8), 24)
        for z in range(4):
            q = sbuf[pl.ds(192 * g + z, 24, stride=8), :]
            dzq = sbuf[pl.ds(192 * g + 4 + z, 24, stride=8), :]
            dyq = dyq_b[z // 2, at_y, LANES * (z % 2) : LANES * (z % 2 + 1)]
            up1 = pltpu.roll(q, LANES - 1, 1)
            up2 = pltpu.roll(q, LANES - 2, 1)
            down1 = pltpu.roll(q, 1, 1)
            qz = jnp.where(comp_n == 0, up2, jnp.where(comp_n == 1, up1, q))
            qy = jnp.where(comp_n == 0, up1, jnp.where(comp_n == 1, q, down1))
            other = jnp.where(real, pltpu.roll(q, LANES - 3, 1), pltpu.roll(q, 3, 1))
            tbuf[pl.ds(z, 24, stride=8), :] = (
                -coef[0, z, at_y, :] * dzq - qz * coef[3, z, at_y, :]
            ) + (
                -coef[1, z, at_y, :] * dyq
                + coef[2, z, at_y, :] * other
                - qy * coef[4, z, at_y, :]
                - lorentz * q
            )
        for h in range(2):
            slot = 2 * g + h
            base = pl.multiple_of(SLOT * slot, 8)
            for i in range(3):
                local = 3 * h + i
                r = 6 * g + local
                t = [tbuf[32 * local + 8 * k : 32 * local + 8 * k + 4, :] for k in range(4)]
                t1 = pltpu.roll(t[1], 96, 1)
                t2 = pltpu.roll(t[2], 64, 1)
                t3 = pltpu.roll(t[3], 32, 1)
                rhs = jnp.concatenate(
                    [
                        jnp.where(lane4 < 96, t[0], t1),
                        jnp.where(lane4 < 64, t1, t2),
                        jnp.where(lane4 < 32, t2, t3),
                    ],
                    axis=1,
                )
                at = pl.ds(pl.multiple_of(384 * r, 128), 384)
                y = 4 * r + lane_y
                mask = jnp.where(z_mask & (y > 0) & (y < N - 1), 1.0, 0.0)
                q = recv_b[pl.ds(pl.multiple_of(8 * r, 8), 4), :]
                acc = mask * (alpha_coef * reg_ref[:, at] + time_step * rhs)
                field = mask * (q + beta_coef * acc)
                a_loc[:, at] = acc
                f_loc[:, at] = field
                for l in range(3):
                    f_buf[pl.ds(base + 12 * i + 4 * l, 4), :] = field[:, 128 * l : 128 * l + 128]

            @pl.when(slot != m)
            def _():
                push(f_buf.at[slot_of(slot), :], g_buf.at[slot_of(m), :], 3, slot, s)

        return carry

    lax.fori_loop(0, M // 2, finish, 0)

    keep(f_buf.at[slot_of(m), :], g_buf.at[slot_of(m), :], 3)
    pick = (iota((16, N), 1) == 12 * m + iota((16, N), 0)).astype(jnp.float32)

    def fold(x):
        x = x + pltpu.roll(x, LANES - 1, 1)
        return x + pltpu.roll(x, LANES - 2, 1)

    here = fold(mm(pick, points))
    there = fold(mm(pick, dpoints))
    which = (iota((16, LANES), 1) // 4) % 3
    back4 = pltpu.roll(here, LANES - 4, 1)
    back8 = pltpu.roll(here, LANES - 8, 1)
    on4 = pltpu.roll(here, 4, 1)
    vel_w = jnp.where(which == 0, back8, jnp.where(which == 1, back4, here))
    vel_v = jnp.where(which == 0, back4, jnp.where(which == 1, here, on4))
    drag = jnp.where(which == 1, 0.0, lorentz_rate)
    dz_here = pltpu.roll(here, LANES - 48, 1)
    tpose[...] = jnp.zeros((LANES, LANES), jnp.float32)
    tpose[0:16, :] = -vel_w * dz_here + (-vel_v * there - drag * here)
    tpose[...] = tpose[...].T
    y_row = 12 * m + iota((1, 12), 1)
    for z in range(4):
        z_row = 4 * s + z
        inside = (y_row > 0) & (y_row < N - 1) & (z_row > 0) & (z_row < N - 1)
        for c in range(3):
            at = 12 * z + 4 * c
            value = tpose[at : at + 1, 0:12]
            outr_ref[c, z : z + 1, :] = time_step * jnp.where(inside, value, 0.0)

    gp[...] = jnp.zeros((2, LANES), jnp.float32)
    arrived(g_buf.at[0 : USED * M, :], 3)
    values = []
    for t in range(9):
        weight_y = wl_ref[t : t + 1, :]
        for z in range(4):
            value = g_buf[pl.ds(4 * t + z, M, stride=SLOT), :]
            values.append(split(value * (weight_y * wz_ref[z : z + 1, :])))
    stack = jnp.concatenate(
        [jnp.concatenate([v[k] for v in values], axis=1) for k in range(3)], axis=0
    )
    nine = lax.dot_general(
        stack, stack, (((1,), (1,)), ((), ())), preferred_element_type=jnp.float32
    )
    three = (nine[2 * M : 3 * M] + nine[M : 2 * M]) + nine[0:M]
    part = (three[:, 2 * M : 3 * M] + three[:, M : 2 * M]) + three[:, 0:M]
    for k in range(M):
        at, lane = divmod(M * k, LANES)
        gp[at : at + 1, lane : lane + M] = part[k : k + 1, :]
    nx, ny = min(4, M), S // 6
    z_hi, x_at = m // nx, lax.rem(m, nx)
    z_lo, y_at, core = s // (2 * ny), lax.rem(s // 2, ny), lax.rem(s, 2)
    mine = (x_at * ny + y_at) * 2 + core
    column, sides = z_lo * ny, (core, 1 - core)
    for dy in FAR[ny]:
        y_to = column + wrap(y_at + dy, ny)
        for dx in sorted(range(nx), key=lambda d: -min(d, nx - d)):
            to = z_hi * nx + wrap(x_at + dx, nx)
            for side in (1, 0):
                if dy or dx or side:
                    push(gp, gr.at[mine], 4, to, y_to * 2 + sides[side])
    keep(gp, gr.at[mine], 4)
    arrived(gr, 4)
    row[...] = jnp.sum(gr[...], axis=0)
    n_hi = M // nx
    level = z_hi * 3 + z_lo
    for dh in sorted(range(n_hi), key=lambda d: -min(d, n_hi - d)):
        to = wrap(z_hi + dh, n_hi) * nx + x_at
        for dl in (1, 2, 0):
            if dh or dl:
                push(row, rows.at[level], 5, to, (wrap(z_lo + dl, 3) * ny + y_at) * 2 + core)
    keep(row, rows.at[level], 5)
    arrived(rows, 5)
    total = jnp.sum(rows[...], axis=0) / CH
    found = jnp.zeros((1, M), jnp.float32)
    for k in range(M):
        at, lane = divmod(M * k, LANES)
        found = jnp.where(m == k, total[at : at + 1, lane : lane + M], found)
    outg_ref[...] = found

    sent(gath_x.at[0 : M - 1], 0)
    sent(recv_b.at[0 : 8 * (S - 1), 0:256], 1)
    sent(recv_b.at[0 : 8 * (S - 1), 256:384], 6)
    sent(recv_c.at[0 : S - 1], 2)
    sent(g_buf.at[0 : USED * (M - 1), :], 3)
    sent(gr.at[0 : 2 * nx * ny - 1], 4)
    sent(rows.at[0 : 3 * n_hi - 1], 5)


def copy_kernel(*refs):
    n = (len(refs) - 1) // 2
    stores = [pltpu.make_async_copy(refs[k], refs[n + k], refs[-1].at[k]) for k in range(n)]
    for store in stores:
        store.start()
    for store in stores:
        store.wait()


def handed_on(arrays):
    n = len(arrays)
    arrays = [pltpu.with_memory_space_constraint(a, pltpu.VMEM) for a in arrays]
    return pl.pallas_call(
        copy_kernel,
        out_shape=[jax.ShapeDtypeStruct(a.shape, a.dtype) for a in arrays],
        in_specs=[pl.BlockSpec(memory_space=pltpu.VMEM)] * n,
        out_specs=[pl.BlockSpec(memory_space=pl.ANY)] * n,
        scratch_shapes=[pltpu.SemaphoreType.DMA((n,))],
        name="hand_on",
    )(*arrays)


def shards(S, M, perturb, register, ref_velocity):
    N = 4 * S
    f32 = jnp.float32
    both, diff_parts, lane_w, z_w = constants(S, M)
    vmem = pl.BlockSpec(memory_space=pltpu.VMEM)
    hbm = pl.BlockSpec(memory_space=pl.ANY)
    outs = pl.pallas_call(
        functools.partial(kernel, S, M),
        out_shape=(
            pltpu.VMEM((4, N * CH), f32),
            pltpu.VMEM((4, N * CH), f32),
            pltpu.VMEM((3, 4, 12), f32),
            pltpu.VMEM((1, M), f32),
        ),
        in_specs=[hbm] * 7,
        out_specs=(vmem,) * 4,
        scratch_shapes=[
            pltpu.VMEM((4 * CH, N), f32),
            pltpu.VMEM((4, N * CH), f32),
            pltpu.VMEM((3, 4, 12), f32),
            pltpu.VMEM((2, 2 * N, N), jnp.bfloat16),
            pltpu.VMEM((2, N, N), jnp.bfloat16),
            pltpu.VMEM((16, LANES), f32),
            pltpu.VMEM((8, LANES), f32),
            pltpu.VMEM((4, 3 * LANES, 4 * LANES), jnp.bfloat16),
            pltpu.VMEM((3 * LANES, 4 * LANES), jnp.bfloat16),
            pltpu.VMEM((2 * N, 384), f32),
            pltpu.VMEM((2 * N, 384), f32),
            pltpu.VMEM((LANES, LANES), f32),
            pltpu.VMEM((4, LANES), f32),
            pltpu.VMEM((M, 4, LANES), f32),
            pltpu.VMEM((N, LANES), f32),
            pltpu.VMEM((N, LANES), f32),
            pltpu.VMEM((S, 1, LANES), f32),
            pltpu.VMEM((S, 1, LANES), f32),
            pltpu.VMEM((5, 4, N, LANES), f32),
            pltpu.VMEM((8 * N, LANES), f32),
            pltpu.VMEM((2, N, 2 * LANES), f32),
            pltpu.VMEM((8 * 24, LANES), f32),
            pltpu.VMEM((SLOT * M, LANES), f32),
            pltpu.VMEM((SLOT * M, LANES), f32),
            pltpu.VMEM((2, LANES), f32),
            pltpu.VMEM((min(4, M) * S // 3, 2, LANES), f32),
            pltpu.VMEM((2, LANES), f32),
            pltpu.VMEM((3 * (M // min(4, M)), 2, LANES), f32),
            pltpu.SemaphoreType.DMA((7,)),
            pltpu.SemaphoreType.DMA((7,)),
            pltpu.SemaphoreType.DMA((7,)),
        ],
        compiler_params=pltpu.CompilerParams(collective_id=0, has_side_effects=True),
        name="substep",
    )(
        perturb.reshape(4 * CH, N),
        register[0],
        ref_velocity,
        jnp.asarray(both),
        jnp.asarray(diff_parts),
        jnp.asarray(lane_w),
        jnp.asarray(z_w),
    )
    fields, acc, ref_step, gram = handed_on(outs)
    return fields[None], acc[None], jnp.transpose(ref_step, (0, 2, 1)), gram


def solution(mesh):
    return jax.shard_map(
        functools.partial(shards, mesh.shape["space"], mesh.shape["member"]),
        mesh=mesh,
        in_specs=(
            P("member", "space", None, None),
            P("member", "space", None),
            P(None, "space", "member"),
        ),
        out_specs=(
            P("member", "space", None),
            P("member", "space", None),
            P(None, "member", "space"),
            P("member", None),
        ),
        check_vma=False,
    )
```

```python
import functools

import jax
import jax.numpy as jnp
import numpy as np
from jax import lax
from jax.experimental import pallas as pl
from jax.experimental.pallas import tpu as pltpu
from jax.sharding import PartitionSpec as P

MESH = pl.DeviceIdType.MESH
HIGHEST = lax.Precision.HIGHEST

time_step = 2e-05
alpha_coef = -5.0 / 9.0
beta_coef = 15.0 / 16.0
lorentz_rate = 25.0
wave_step = 0.5

CH = 96
LANES = 128
SLOT = 40
USED = 36
EXPAND = 6
FAR = {8: (4, 3, 5, 2, 6, 1, 7, 0), 1: (0,)}


def cheb_matrix(points):
    intervals = points - 1
    index = np.arange(points)
    nodes = np.cos(np.pi * index / intervals)
    signs = np.ones(points)
    signs[0] = 2.0
    signs[-1] = 2.0
    signs = signs * (-1.0) ** index
    spread = nodes[:, None] - nodes[None, :]
    matrix = signs[:, None] / signs[None, :] / (spread + np.eye(points))
    matrix = matrix - np.eye(points) * matrix.sum(axis=1)[:, None]
    return matrix


def quad_weights(points):
    index = np.arange(points)
    return np.pi / (points - 1) * np.sin(np.pi * index / (points - 1))


def parts_of(matrix):
    hi = matrix.astype(jnp.bfloat16)
    mid = (matrix - hi.astype(np.float32)).astype(jnp.bfloat16)
    return np.stack([hi, mid])


def constants(space, members):
    points = 4 * space
    diff = cheb_matrix(points).astype(np.float32)
    both = np.stack([np.eye(points, dtype=np.float32), diff]).reshape(2, space, 4, points)
    both = both.transpose(1, 0, 2, 3).reshape(2 * points, points)
    weight = quad_weights(points)
    root = np.sqrt(np.maximum(weight, 0.0))
    lane_w = np.zeros((members, 16, LANES), np.float32)
    lane_w[:, :9] = np.repeat(root, CH).reshape(members, 9, LANES)
    z_w = np.zeros((space, 8, LANES), np.float32)
    z_w[:, :4] = root.reshape(space, 4, 1)
    return parts_of(both), parts_of(diff), lane_w, z_w


def mm(a, b, transpose_b=False):
    dims = (((1,), (1 if transpose_b else 0,)), ((), ()))
    return lax.dot_general(a, b, dims, precision=HIGHEST, preferred_element_type=jnp.float32)


def split(x):
    hi = x.astype(jnp.bfloat16)
    rest = x - hi.astype(jnp.float32)
    mid = rest.astype(jnp.bfloat16)
    lo = (rest - mid.astype(jnp.float32)).astype(jnp.bfloat16)
    return hi, mid, lo


def mm_bf(a, b, contract_b=0):
    dims = (((1,), (contract_b,)), ((), ()))
    return lax.dot_general(a, b, dims, preferred_element_type=jnp.float32)


def mm_exact(parts, b):
    return mm_bf(jnp.concatenate(parts, axis=1), b)


def iota(shape, axis):
    return lax.broadcasted_iota(jnp.int32, shape, axis)


def kernel(
    S,
    M,
    p_hbm,
    reg_hbm,
    v_hbm,
    a_hbm,
    dp_hbm,
    wl_hbm,
    wz_hbm,
    f_loc,
    a_loc,
    outr_ref,
    outg_ref,
    p_ref,
    reg_ref,
    v_ref,
    a_ref,
    dp_ref,
    wl_ref,
    wz_ref,
    sel_p,
    sel_d,
    send_b,
    recv_b,
    tpose,
    own_x,
    gath_x,
    xz,
    ct,
    send_c,
    recv_c,
    coef,
    sbuf,
    dyq_b,
    tbuf,
    f_buf,
    g_buf,
    gp,
    gr,
    row,
    rows,
    send_sem,
    recv_sem,
    in_sem,
):
    N = 4 * S
    H = S // 2
    m = lax.axis_index("member")
    s = lax.axis_index("space")

    def wrap(value, size):
        return jnp.where(value >= size, value - size, value)

    def over_space(body):
        def step(k, carry):
            body(wrap(s + k, S))
            body(wrap(s + S - k, S))
            return carry

        lax.fori_loop(1, H, step, 0)
        body(wrap(s + H, S))

    def far_space(body):
        ny = S // 6
        core = lax.rem(s, 2)
        y = lax.rem(s // 2, ny)
        z = s // (2 * ny)

        def step(k, carry):
            column = wrap(z + lax.rem(k, 3), 3) * ny
            side = wrap(core + k // 3, 2)
            for dy in FAR[ny]:
                t = (column + wrap(y + dy, ny)) * 2 + side
                if dy == 0:

                    @pl.when(k != 0)
                    def _():
                        body(t)

                else:
                    body(t)
            return carry

        lax.fori_loop(0, 6, step, 0)

    def each_space(body):
        ny = S // 6
        core = lax.rem(s, 2)
        y = lax.rem(s // 2, ny)
        z = s // (2 * ny)
        columns = [wrap(z + dz, 3) * ny for dz in range(3)]
        sides = [core, 1 - core]
        for dy in FAR[ny]:
            at = wrap(y + dy, ny)
            for dz in (1, 2, 0):
                for side in (1, 0):
                    if dy or dz or side:
                        body((columns[dz] + at) * 2 + sides[side])

    def over_member(body):
        for k in range(1, M):
            body(wrap(m + k, M))

    def push(src, dst, which, member, space):
        pltpu.make_async_remote_copy(
            src_ref=src,
            dst_ref=dst,
            send_sem=send_sem.at[which],
            recv_sem=recv_sem.at[which],
            device_id=(member, space),
            device_id_type=MESH,
        ).start()

    def keep(src, dst, which):
        pltpu.make_async_copy(src, dst, recv_sem.at[which]).start()

    def arrived(ref, which):
        pltpu.make_async_copy(ref, ref, recv_sem.at[which]).wait()

    def sent(ref, which):
        pltpu.make_async_copy(ref, ref, send_sem.at[which]).wait()

    loads = [
        pltpu.make_async_copy(src, dst, in_sem.at[k])
        for k, (src, dst) in enumerate(
            (
                (v_hbm, v_ref),
                (p_hbm, p_ref),
                (a_hbm, a_ref),
                (dp_hbm, dp_ref),
                (reg_hbm, reg_ref),
                (wl_hbm.at[m], wl_ref),
                (wz_hbm.at[s], wz_ref),
            )
        )
    ]
    for load in loads:
        load.start()

    barrier = pltpu.get_barrier_semaphore()
    each_space(
        lambda t: pl.semaphore_signal(barrier, inc=1, device_id=(m, t), device_id_type=MESH)
    )
    over_member(
        lambda t: pl.semaphore_signal(barrier, inc=1, device_id=(t, s), device_id_type=MESH)
    )

    tpose[...] = jnp.zeros((LANES, LANES), jnp.float32)
    loads[0].wait()
    for c in range(3):
        tpose[4 * c : 4 * c + 4, 0:12] = v_ref[c]
    tpose[...] = tpose[...].T
    own_x[...] = (
        tpose[0:4, :]
        + pltpu.roll(tpose[4:8, :], 12, 1)
        + pltpu.roll(tpose[8:12, :], 24, 1)
    )
    loads[1].wait()
    loads[2].wait()
    q_hi, q_mid, q_lo = split(p_ref[...])
    send_b[...] = (
        (mm_bf(a_ref[0], q_lo, 1) + mm_bf(a_ref[1], q_hi, 1)) + mm_bf(a_ref[0], q_mid, 1)
    ) + mm_bf(a_ref[0], q_hi, 1)
    pl.semaphore_wait(barrier, S - 1 + M - 1)

    over_member(lambda t: push(own_x, gath_x.at[m], 0, t, s))
    keep(own_x, gath_x.at[m], 0)

    def bulk(first, last, which):
        mine = pl.ds(pl.multiple_of(8 * s, 8), 8)
        lanes = slice(first, last)

        def one(t):
            push(
                send_b.at[pl.ds(pl.multiple_of(8 * t, 8), 8), lanes],
                recv_b.at[mine, lanes],
                which,
                m,
                t,
            )

        far_space(one)
        keep(send_b.at[mine, lanes], recv_b.at[mine, lanes], which)

    bulk(0, 256, 1)

    group = iota((LANES, LANES), 0) // 4
    lane = iota((LANES, LANES), 1)
    comp = lane % 3
    kx = wave_step * (lane // 6 + 1).astype(jnp.float32)
    kx = jnp.where(lane % 6 < 3, kx, -kx)
    for z in range(4):
        chosen = [
            (group == 3 * z + 2).astype(jnp.float32),
            (group == 3 * z + 1).astype(jnp.float32),
            jnp.where(group == 3 * z, kx, 0.0),
            (group == 12 + 3 * z + comp).astype(jnp.float32),
        ]
        for k in range(4):
            one = chosen[k].astype(jnp.bfloat16)
            for i in range(3):
                sel_p[z, LANES * i : LANES * (i + 1), LANES * k : LANES * (k + 1)] = one
        one = (group == 3 * z + comp).astype(jnp.float32).astype(jnp.bfloat16)
        for i in range(3):
            sel_d[LANES * i : LANES * (i + 1), LANES * z : LANES * (z + 1)] = one
    for load in loads[3:]:
        load.wait()

    arrived(gath_x, 0)
    for k in range(M):
        piece = gath_x[k]
        for j in range(3):
            part = piece if j == 0 else pltpu.roll(piece, LANES - 12 * j, 1)
            xz[12 * k + 4 * j : 12 * k + 4 * j + 4, :] = part
    x = jnp.where(iota((N, LANES), 1) < 12, xz[...], 0.0)
    xz[...] = x
    def slope(parts):
        hi, mid, lo = parts
        return (
            (mm_bf(dp_ref[0], lo) + mm_bf(dp_ref[1], mid))
            + (mm_bf(dp_ref[0], mid) + mm_bf(dp_ref[1], hi))
        ) + mm_bf(dp_ref[0], hi)

    ct[...] = slope(split(x))
    packed = xz[pl.ds(0, S, stride=4), :]
    for z in range(1, 4):
        packed = packed + pltpu.roll(xz[pl.ds(z, S, stride=4), :], 12 * z, 1)
    for z in range(4):
        packed = packed + pltpu.roll(ct[pl.ds(z, S, stride=4), :], 48 + 12 * z, 1)
    send_c[:, 0, :] = packed
    over_space(lambda t: push(send_c.at[t], recv_c.at[s], 2, m, t))
    keep(send_c.at[s], recv_c.at[s], 2)
    bulk(256, 384, 6)

    lane8 = iota((8, LANES), 1)

    def expand(last):
        def go(step, carry):
            for u in range(EXPAND):
                r = EXPAND * step + u
                base = pl.ds(pl.multiple_of(8 * r, 8), 8)
                v1 = recv_b[base, 128:256]
                if last:
                    v2 = recv_b[base, 256:384]
                    tiles = (
                        jnp.where(lane8 < 64, pltpu.roll(v1, 64, 1), pltpu.roll(v2, 64, 1)),
                        pltpu.roll(v2, 96, 1),
                    )
                else:
                    v0 = recv_b[base, 0:128]
                    tiles = (
                        v0,
                        jnp.where(lane8 < 32, pltpu.roll(v0, 32, 1), pltpu.roll(v1, 32, 1)),
                    )
                for i, v in enumerate(tiles):
                    at = 32 * r + 8 * (i + 2 * last)
                    sbuf[pl.ds(pl.multiple_of(at, 8), 8), :] = v
            return carry

        lax.fori_loop(0, S // EXPAND, go, 0)

    arrived(recv_b.at[:, 0:256], 1)
    expand(0)

    arrived(recv_c, 2)
    lane_s = iota((S, LANES), 1) % 4
    for k in range(4):
        xz[pl.ds(k, S, stride=4), :] = jnp.where(lane_s == k, recv_c[:, 0, :], 0.0)
    points = xz[...]
    parts = split(points)
    dpoints = slope(parts)
    spread_y = mm_exact(split(dpoints), sel_d[...])
    for z in range(4):
        spread_p = mm_exact(parts, sel_p[z])
        for k in range(4):
            coef[k, z] = spread_p[:, LANES * k : LANES * (k + 1)]
        coef[4, z] = spread_y[:, LANES * z : LANES * (z + 1)]


    arrived(recv_b.at[:, 256:384], 6)
    expand(1)
    for pair in range(2):
        q2 = jnp.concatenate(
            [sbuf[pl.ds(2 * pair + i, N, stride=8), :] for i in range(2)], axis=1
        )
        q_hi, q_mid, _ = split(q2)
        dyq_b[pair] = (mm_bf(dp_ref[0], q_mid) + mm_bf(dp_ref[1], q_hi)) + mm_bf(dp_ref[0], q_hi)

    lane_n = iota((24, LANES), 1)
    lorentz = jnp.where(lane_n % 3 == 1, 0.0, lorentz_rate)
    real = lane_n % 6 < 3
    comp_n = lane_n % 3
    lane4 = iota((4, LANES), 1)
    z_rows = 4 * s + iota((4, 384), 0)
    z_mask = (z_rows > 0) & (z_rows < N - 1)
    lane_y = iota((4, 384), 1) // CH

    def slot_of(t):
        return pl.ds(pl.multiple_of(SLOT * t, 8), USED)

    def finish(step, carry):
        if M == 16:
            off = jnp.where(step < 4, step + 4, jnp.where(step < 6, step - 2, step - 6))
        else:
            off = step
        g = wrap(m // 2 + off, M // 2)
        at_y = pl.ds(pl.multiple_of(24 * g, 8), 24)
        for z in range(4):
            q = sbuf[pl.ds(192 * g + z, 24, stride=8), :]
            dzq = sbuf[pl.ds(192 * g + 4 + z, 24, stride=8), :]
            dyq = dyq_b[z // 2, at_y, LANES * (z % 2) : LANES * (z % 2 + 1)]
            up1 = pltpu.roll(q, LANES - 1, 1)
            up2 = pltpu.roll(q, LANES - 2, 1)
            down1 = pltpu.roll(q, 1, 1)
            qz = jnp.where(comp_n == 0, up2, jnp.where(comp_n == 1, up1, q))
            qy = jnp.where(comp_n == 0, up1, jnp.where(comp_n == 1, q, down1))
            other = jnp.where(real, pltpu.roll(q, LANES - 3, 1), pltpu.roll(q, 3, 1))
            tbuf[pl.ds(z, 24, stride=8), :] = (
                -coef[0, z, at_y, :] * dzq - qz * coef[3, z, at_y, :]
            ) + (
                -coef[1, z, at_y, :] * dyq
                + coef[2, z, at_y, :] * other
                - qy * coef[4, z, at_y, :]
                - lorentz * q
            )
        for h in range(2):
            slot = 2 * g + h
            base = pl.multiple_of(SLOT * slot, 8)
            for i in range(3):
                local = 3 * h + i
                r = 6 * g + local
                t = [tbuf[32 * local + 8 * k : 32 * local + 8 * k + 4, :] for k in range(4)]
                t1 = pltpu.roll(t[1], 96, 1)
                t2 = pltpu.roll(t[2], 64, 1)
                t3 = pltpu.roll(t[3], 32, 1)
                rhs = jnp.concatenate(
                    [
                        jnp.where(lane4 < 96, t[0], t1),
                        jnp.where(lane4 < 64, t1, t2),
                        jnp.where(lane4 < 32, t2, t3),
                    ],
                    axis=1,
                )
                at = pl.ds(pl.multiple_of(384 * r, 128), 384)
                y = 4 * r + lane_y
                mask = jnp.where(z_mask & (y > 0) & (y < N - 1), 1.0, 0.0)
                q = recv_b[pl.ds(pl.multiple_of(8 * r, 8), 4), :]
                acc = mask * (alpha_coef * reg_ref[:, at] + time_step * rhs)
                field = mask * (q + beta_coef * acc)
                a_loc[:, at] = acc
                f_loc[:, at] = field
                for l in range(3):
                    f_buf[pl.ds(base + 12 * i + 4 * l, 4), :] = field[:, 128 * l : 128 * l + 128]

            @pl.when(slot != m)
            def _():
                push(f_buf.at[slot_of(slot), :], g_buf.at[slot_of(m), :], 3, slot, s)

        return carry

    lax.fori_loop(0, M // 2, finish, 0)

    keep(f_buf.at[slot_of(m), :], g_buf.at[slot_of(m), :], 3)
    pick = (iota((16, N), 1) == 12 * m + iota((16, N), 0)).astype(jnp.float32)

    def fold(x):
        x = x + pltpu.roll(x, LANES - 1, 1)
        return x + pltpu.roll(x, LANES - 2, 1)

    here = fold(mm(pick, points))
    there = fold(mm(pick, dpoints))
    which = (iota((16, LANES), 1) // 4) % 3
    back4 = pltpu.roll(here, LANES - 4, 1)
    back8 = pltpu.roll(here, LANES - 8, 1)
    on4 = pltpu.roll(here, 4, 1)
    vel_w = jnp.where(which == 0, back8, jnp.where(which == 1, back4, here))
    vel_v = jnp.where(which == 0, back4, jnp.where(which == 1, here, on4))
    drag = jnp.where(which == 1, 0.0, lorentz_rate)
    dz_here = pltpu.roll(here, LANES - 48, 1)
    tpose[...] = jnp.zeros((LANES, LANES), jnp.float32)
    tpose[0:16, :] = -vel_w * dz_here + (-vel_v * there - drag * here)
    tpose[...] = tpose[...].T
    y_row = 12 * m + iota((1, 12), 1)
    for z in range(4):
        z_row = 4 * s + z
        inside = (y_row > 0) & (y_row < N - 1) & (z_row > 0) & (z_row < N - 1)
        for c in range(3):
            at = 12 * z + 4 * c
            value = tpose[at : at + 1, 0:12]
            outr_ref[c, z : z + 1, :] = time_step * jnp.where(inside, value, 0.0)

    gp[...] = jnp.zeros((2, LANES), jnp.float32)
    arrived(g_buf.at[0 : USED * M, :], 3)
    values = []
    for t in range(9):
        weight_y = wl_ref[t : t + 1, :]
        for z in range(4):
            value = g_buf[pl.ds(4 * t + z, M, stride=SLOT), :]
            values.append(split(value * (weight_y * wz_ref[z : z + 1, :])))
    stack = jnp.concatenate(
        [jnp.concatenate([v[k] for v in values], axis=1) for k in range(2)], axis=0
    )
    four = lax.dot_general(
        stack, stack, (((1,), (1,)), ((), ())), preferred_element_type=jnp.float32
    )
    two = four[M : 2 * M] + four[0:M]
    part = two[:, M : 2 * M] + two[:, 0:M]
    for k in range(M):
        at, lane = divmod(M * k, LANES)
        gp[at : at + 1, lane : lane + M] = part[k : k + 1, :]
    nx, ny = min(4, M), S // 6
    z_hi, x_at = m // nx, lax.rem(m, nx)
    z_lo, y_at, core = s // (2 * ny), lax.rem(s // 2, ny), lax.rem(s, 2)
    mine = (x_at * ny + y_at) * 2 + core
    column, sides = z_lo * ny, (core, 1 - core)
    for dy in FAR[ny]:
        y_to = column + wrap(y_at + dy, ny)
        for dx in sorted(range(nx), key=lambda d: -min(d, nx - d)):
            to = z_hi * nx + wrap(x_at + dx, nx)
            for side in (1, 0):
                if dy or dx or side:
                    push(gp, gr.at[mine], 4, to, y_to * 2 + sides[side])
    keep(gp, gr.at[mine], 4)
    arrived(gr, 4)
    row[...] = jnp.sum(gr[...], axis=0)
    n_hi = M // nx
    level = z_hi * 3 + z_lo
    for dh in sorted(range(n_hi), key=lambda d: -min(d, n_hi - d)):
        to = wrap(z_hi + dh, n_hi) * nx + x_at
        for dl in (1, 2, 0):
            if dh or dl:
                push(row, rows.at[level], 5, to, (wrap(z_lo + dl, 3) * ny + y_at) * 2 + core)
    keep(row, rows.at[level], 5)
    arrived(rows, 5)
    total = jnp.sum(rows[...], axis=0) / CH
    found = jnp.zeros((1, M), jnp.float32)
    for k in range(M):
        at, lane = divmod(M * k, LANES)
        found = jnp.where(m == k, total[at : at + 1, lane : lane + M], found)
    outg_ref[...] = found

    sent(gath_x.at[0 : M - 1], 0)
    sent(recv_b.at[0 : 8 * (S - 1), 0:256], 1)
    sent(recv_b.at[0 : 8 * (S - 1), 256:384], 6)
    sent(recv_c.at[0 : S - 1], 2)
    sent(g_buf.at[0 : USED * (M - 1), :], 3)
    sent(gr.at[0 : 2 * nx * ny - 1], 4)
    sent(rows.at[0 : 3 * n_hi - 1], 5)


def copy_kernel(*refs):
    n = (len(refs) - 1) // 2
    stores = [pltpu.make_async_copy(refs[k], refs[n + k], refs[-1].at[k]) for k in range(n)]
    for store in stores:
        store.start()
    for store in stores:
        store.wait()


def handed_on(arrays):
    n = len(arrays)
    arrays = [pltpu.with_memory_space_constraint(a, pltpu.VMEM) for a in arrays]
    return pl.pallas_call(
        copy_kernel,
        out_shape=[jax.ShapeDtypeStruct(a.shape, a.dtype) for a in arrays],
        in_specs=[pl.BlockSpec(memory_space=pltpu.VMEM)] * n,
        out_specs=[pl.BlockSpec(memory_space=pl.ANY)] * n,
        scratch_shapes=[pltpu.SemaphoreType.DMA((n,))],
        name="hand_on",
    )(*arrays)


def shards(S, M, perturb, register, ref_velocity):
    N = 4 * S
    f32 = jnp.float32
    both, diff_parts, lane_w, z_w = constants(S, M)
    vmem = pl.BlockSpec(memory_space=pltpu.VMEM)
    hbm = pl.BlockSpec(memory_space=pl.ANY)
    outs = pl.pallas_call(
        functools.partial(kernel, S, M),
        out_shape=(
            pltpu.VMEM((4, N * CH), f32),
            pltpu.VMEM((4, N * CH), f32),
            pltpu.VMEM((3, 4, 12), f32),
            pltpu.VMEM((1, M), f32),
        ),
        in_specs=[hbm] * 7,
        out_specs=(vmem,) * 4,
        scratch_shapes=[
            pltpu.VMEM((4 * CH, N), f32),
            pltpu.VMEM((4, N * CH), f32),
            pltpu.VMEM((3, 4, 12), f32),
            pltpu.VMEM((2, 2 * N, N), jnp.bfloat16),
            pltpu.VMEM((2, N, N), jnp.bfloat16),
            pltpu.VMEM((16, LANES), f32),
            pltpu.VMEM((8, LANES), f32),
            pltpu.VMEM((4, 3 * LANES, 4 * LANES), jnp.bfloat16),
            pltpu.VMEM((3 * LANES, 4 * LANES), jnp.bfloat16),
            pltpu.VMEM((2 * N, 384), f32),
            pltpu.VMEM((2 * N, 384), f32),
            pltpu.VMEM((LANES, LANES), f32),
            pltpu.VMEM((4, LANES), f32),
            pltpu.VMEM((M, 4, LANES), f32),
            pltpu.VMEM((N, LANES), f32),
            pltpu.VMEM((N, LANES), f32),
            pltpu.VMEM((S, 1, LANES), f32),
            pltpu.VMEM((S, 1, LANES), f32),
            pltpu.VMEM((5, 4, N, LANES), f32),
            pltpu.VMEM((8 * N, LANES), f32),
            pltpu.VMEM((2, N, 2 * LANES), f32),
            pltpu.VMEM((8 * 24, LANES), f32),
            pltpu.VMEM((SLOT * M, LANES), f32),
            pltpu.VMEM((SLOT * M, LANES), f32),
            pltpu.VMEM((2, LANES), f32),
            pltpu.VMEM((min(4, M) * S // 3, 2, LANES), f32),
            pltpu.VMEM((2, LANES), f32),
            pltpu.VMEM((3 * (M // min(4, M)), 2, LANES), f32),
            pltpu.SemaphoreType.DMA((7,)),
            pltpu.SemaphoreType.DMA((7,)),
            pltpu.SemaphoreType.DMA((7,)),
        ],
        compiler_params=pltpu.CompilerParams(collective_id=0, has_side_effects=True),
        name="substep",
    )(
        perturb.reshape(4 * CH, N),
        register[0],
        ref_velocity,
        jnp.asarray(both),
        jnp.asarray(diff_parts),
        jnp.asarray(lane_w),
        jnp.asarray(z_w),
    )
    fields, acc, ref_step, gram = handed_on(outs)
    return fields[None], acc[None], jnp.transpose(ref_step, (0, 2, 1)), gram


def solution(mesh):
    return jax.shard_map(
        functools.partial(shards, mesh.shape["space"], mesh.shape["member"]),
        mesh=mesh,
        in_specs=(
            P("member", "space", None, None),
            P("member", "space", None),
            P(None, "space", "member"),
        ),
        out_specs=(
            P("member", "space", None),
            P("member", "space", None),
            P(None, "member", "space"),
            P("member", None),
        ),
        check_vma=False,
    )
```
